128 devices in a mesh: seq: 32 (over x, z, core), tm: 4 (over y).
Axes of the slice: x: 4, y: 4, z: 4, core: 2. Of those that a mesh axis runs over, the one named last changes fastest.
Arguments:
- latent: bfloat16 [8, 16384], P(None, ('seq', 'tm')), may hold values from -6 to 6
- first_kernel: bfloat16 [3, 3, 3, 16, 512], replicated, may hold values from -0.3125 to 0.3125
- first_bias: float32 [512], replicated, may hold values from -3 to 3
- first_gain: float32 [512], replicated, may hold values from 0.1 to 1.9
- second_kernel: bfloat16 [3, 3, 3, 512, 256], replicated, may hold values from -0.0546875 to 0.0546875
- second_bias: float32 [256], replicated, may hold values from -3 to 3
- second_gain: float32 [256], replicated, may hold values from 0.1 to 1.9
- final_kernel: bfloat16 [3, 3, 3, 256, 128], replicated, may hold values from -0.078125 to 0.078125
- final_bias: float32 [128], replicated, may hold values from -2 to 2
Outputs:
- decoded: bfloat16 [8, 128, 128, 128], P('tm', 'seq')
The draws below stay inside these ranges and needn't reach their ends.
All inputs are finite; a program needn't handle non-finite values.
Results may differ from the reference program's by a relative error of at most 0.0051.
Values may be sent and summed in bfloat16 or wider, within the bound.
A program may use at most 64 MiB of HBM per device.

```python
import jax
import jax.numpy as jnp
from jax import lax

CL = 16
C1 = 512
C2 = 256
C3 = 128
W = 32
FRAMES = 8
ROWS = 32


def block_levels(key, dims, pieces, low, top_value):
    level, own = 1.0, jax.random.fold_in(key, 6)
    for dim, blocks in pieces:
        steps = jnp.exp(jax.random.uniform(jax.random.fold_in(own, dim), (blocks,), jnp.float32, low / len(pieces), top_value / len(pieces)))
        level = level * jnp.repeat(steps, dims[dim] // blocks).reshape([-1 if axis == dim else 1 for axis in range(len(dims))])
    return level


def normal_values(key, extent, deviation, most, pieces=(), held_as=jnp.bfloat16):
    gain = block_levels(key, extent, pieces, -0.22, 0.18) if pieces else 1.0
    entries = jax.random.normal(key, extent, jnp.float32) * deviation * gain
    return jnp.minimum(jnp.maximum(entries, -most), most).astype(held_as)


def setup_inputs(seed: int = 0) -> dict:
    seeds = jax.random.split(jax.random.key(seed), 10)
    return {
        "latent": normal_values(seeds[0], (FRAMES, ROWS * W * CL), 1.0, 6.0, ((1, 128),)),
        "first_kernel": normal_values(seeds[1], (3, 3, 3, CL, C1), (27 * CL) ** -0.5, 0.3125),
        "first_bias": normal_values(seeds[2], (C1,), 0.5, 3.0, (), jnp.float32),
        "first_gain": jnp.clip(1.0 + 0.18 * jax.random.normal(seeds[3], (C1,), jnp.float32), 0.1, 1.9),
        "second_kernel": normal_values(seeds[4], (3, 3, 3, C1, C2), (27 * C1) ** -0.5, 0.0546875),
        "second_bias": normal_values(seeds[5], (C2,), 0.5, 3.0, (), jnp.float32),
        "second_gain": jnp.clip(1.0 + 0.18 * jax.random.normal(seeds[6], (C2,), jnp.float32), 0.1, 1.9),
        "final_kernel": normal_values(seeds[7], (3, 3, 3, C2, C3), (27 * C2) ** -0.5, 0.078125),
        "final_bias": normal_values(seeds[8], (C3,), 0.3, 2.0, (), jnp.float32),
    }


def edge_conv(field, kernel, offset):
    padded = jnp.pad(field, ((2, 0), (1, 1), (1, 1), (0, 0)), mode='edge')
    result = lax.conv_general_dilated(padded[None], kernel.astype(jnp.float32), (1, 1, 1), 'VALID', dimension_numbers=('NDHWC', 'DHWIO', 'NDHWC'), precision=lax.Precision.HIGHEST)
    return result[0] + offset

def normed(hidden, norm_gain):
    factor = lax.rsqrt(lax.optimization_barrier(jnp.mean(hidden * hidden, axis=3, keepdims=True)) + 1e-06)
    return jax.nn.silu(hidden * factor * norm_gain).astype(jnp.bfloat16)

def enlarge(field):
    return jnp.repeat(jnp.repeat(field, 2, axis=1), 2, axis=2)

def reference(latent, first_kernel, first_bias, first_gain, second_kernel, second_bias, second_gain, final_kernel, final_bias):
    latent_grid = latent.reshape(FRAMES, ROWS, W, CL).astype(jnp.float32)
    first_act = normed(edge_conv(latent_grid, first_kernel, first_bias), first_gain)
    second_act = normed(edge_conv(enlarge(first_act.astype(jnp.float32)), second_kernel, second_bias), second_gain)
    decoded = edge_conv(enlarge(second_act.astype(jnp.float32)), final_kernel, final_bias)
    return decoded.astype(jnp.bfloat16)
```

```python
import functools

import jax
import jax.numpy as jnp
from jax import lax
from jax.experimental import pallas as pl
from jax.experimental.pallas import tpu as pltpu
from jax.sharding import PartitionSpec as P

MESH = pl.DeviceIdType.MESH
F32 = jnp.float32
BF16 = jnp.bfloat16

SEQ = 32
TM = 4
W = 32
C1, C2, C3 = 512, 256, 128
EPS = 1e-06

CORNERS = ((0, 0), (0, 2), (2, 0), (2, 2))
OTHERS = ((0, 1), (1, 0), (1, 1), (1, 2), (2, 1))


def gather_kernel(x_ref, lat_ref, send_sem, recv_sem, own_sem):
    s, t = lax.axis_index("seq"), lax.axis_index("tm")
    peers = [(d, e) for d in (0, 1, -1, 2, -2) for e in range(TM) if (d, e) != (0, 0)]

    def where(d, e):
        return (lax.rem(s + (d + SEQ), SEQ), lax.rem(t + e, TM))

    barrier = pltpu.get_barrier_semaphore()
    for d, e in peers:
        pl.semaphore_signal(barrier, inc=1, device_id=where(d, e), device_id_type=MESH)
    own = pltpu.make_async_copy(x_ref, lat_ref.at[2, t], own_sem)
    own.start()
    pl.semaphore_wait(barrier, len(peers))
    copies = []
    for n, (d, e) in enumerate(peers):
        slot = 2 - d
        copy = pltpu.make_async_remote_copy(
            src_ref=x_ref,
            dst_ref=lat_ref.at[slot, t],
            send_sem=send_sem.at[n],
            recv_sem=recv_sem.at[slot, t],
            device_id=where(d, e),
            device_id_type=MESH,
        )
        copy.start()
        copies.append(copy)
    own.wait()
    for d, e in peers:
        frm = lax.rem(t + e, TM)
        pltpu.make_async_remote_copy(
            src_ref=x_ref,
            dst_ref=lat_ref.at[2 + d, frm],
            send_sem=send_sem.at[0],
            recv_sem=recv_sem.at[2 + d, frm],
            device_id=where(d, e),
            device_id_type=MESH,
        ).wait_recv()
    for copy in copies:
        copy.wait_send()


def gather_rows(latent):
    return pl.pallas_call(
        gather_kernel,
        out_shape=jax.ShapeDtypeStruct((5, TM, 8, 128), BF16),
        in_specs=[pl.BlockSpec(memory_space=pltpu.VMEM)],
        out_specs=pl.BlockSpec(memory_space=pltpu.VMEM),
        scratch_shapes=[
            pltpu.SemaphoreType.DMA((19,)),
            pltpu.SemaphoreType.DMA((5, TM)),
            pltpu.SemaphoreType.DMA,
        ],
        compiler_params=pltpu.CompilerParams(collective_id=0, has_side_effects=True),
        name="gather_rows",
    )(latent)


def silu_normed(hidden, gain):
    factor = lax.rsqrt(jnp.mean(hidden * hidden, axis=1, keepdims=True) + EPS)
    v = hidden * factor * gain
    half = 0.5 * v
    return (half + half * jnp.tanh(half)).astype(BF16)


def patches(lat_ref, pat_ref, s, t):
    late = 6 - 2 * t
    sub = lax.broadcasted_iota(jnp.int32, (8, 128), 0)
    lane = lax.broadcasted_iota(jnp.int32, (8, 128), 1)
    turned = []
    for q in range(5):
        row = jnp.clip(s - 2 + q, 0, SEQ - 1) - s + 2
        blocks = []
        for b in range(TM):
            x = lat_ref[row, b].astype(F32)
            moved = pltpu.roll(x, late, 0)
            x = jnp.where(sub < late, jnp.broadcast_to(x[0:1], (8, 128)), moved)
            blocks.append([pltpu.roll(x, (128 - 16 * (m - 1)) % 128, 1) for m in range(8)])
        turned.append(blocks)

    def piece(q, c, up):
        b, m = c // 8, c % 8
        k = (m + 4) % 8 if up else m
        base = 64 if up else 0
        own = turned[q][b][k]
        if m == 0:
            other = turned[q][b - 1][k] if b else turned[q][0][(k + 1) % 8]
            own = jnp.where(lane < base + 16, other, own)
        if m == 7:
            other = turned[q][b + 1][k] if b < 3 else turned[q][3][(k + 7) % 8]
            own = jnp.where(lane >= base + 32, other, own)
        return own

    for q in range(5):
        for c in range(W):
            low = piece(q, c, False)
            if q < 4:
                high = jnp.where((lane >= 64) & (lane < 112), piece(q + 1, c, True), 0.0)
            else:
                high = jnp.zeros((8, 128), F32)
            pat_ref[q, pl.ds(c, 8, stride=W), :] = jnp.where(lane < 48, low, high)


def sums(taps):
    r12 = [taps[1, k] + taps[2, k] for k in range(3)]
    r01 = [taps[0, k] + taps[1, k] for k in range(3)]
    k0 = [taps[0, k] for k in range(3)]
    k2 = [taps[2, k] for k in range(3)]
    total = lambda r: r[0] + r[1] + r[2]
    return {
        (0, 0, 1): total(k0),
        (0, 1, 0): r12[0],
        (0, 1, 1): total(r12),
        (0, 1, 2): r12[2],
        (1, 0, 0): r01[0],
        (1, 0, 1): total(r01),
        (1, 0, 2): r01[2],
        (1, 1, 1): total(k2),
    }


def corner_place(j, k):
    return (0, 0, k) if j == 0 else (1, 1, k)


def decode_kernel(
    lat_ref, w1_hbm, b1_ref, g1_ref, w2_hbm, b2_ref, g2_ref, w3_hbm, b3_ref,
    out_ref,
    w1, w2c, w2r, w3c, w3r, pat, x1, x2, o32, sem1, sem2, sem3,
):
    s, t = lax.axis_index("seq"), lax.axis_index("tm")

    copies1, copies2, copies3 = [], [[], [], []], []
    for i in range(3):
        for j in range(3):
            start = 256 * i + 64 * j
            copies1.append(
                pltpu.make_async_copy(w1_hbm.at[i, j], w1.at[pl.ds(start, 48), :], sem1.at[i, j])
            )
    for i in range(3):
        for j, k in CORNERS + OTHERS:
            if (j, k) in CORNERS:
                rp, u, b = corner_place(j, k)
                d2 = w2c.at[rp, b, u, i]
                d3 = w3c.at[rp, u, i, :, pl.ds(C3 * b, C3)]
            else:
                n = OTHERS.index((j, k))
                d2, d3 = w2r.at[i, n], w3r.at[i, n]
            copies2[i].append(pltpu.make_async_copy(w2_hbm.at[i, j, k], d2, sem2.at[i, j, k]))
            copies3.append(pltpu.make_async_copy(w3_hbm.at[i, j, k], d3, sem3.at[i, j, k]))
    zeros = jnp.zeros((16, C1), BF16)
    for i in range(3):
        for start in (48, 112, 176, 192, 208, 224, 240):
            w1[256 * i + start : 256 * i + start + 16, :] = zeros
    for copy in copies1 + copies2[0] + copies2[1] + copies2[2] + copies3:
        copy.start()

    patches(lat_ref, pat, s, t)
    lhs = []
    for r in range(3):
        q = jnp.clip(s - 1 + r, 0, SEQ - 1) - s + 1
        cols = []
        for i in range(3):
            for two in (0, 2):
                cols.append(pat[q + two, 32 * i : 32 * i + 192, :].astype(BF16))
        lhs.append(jnp.concatenate(cols, axis=1))
    lhs = jnp.concatenate(lhs, axis=0)
    for copy in copies1:
        copy.wait()
    hidden = jnp.dot(lhs, w1[...], preferred_element_type=F32) + b1_ref[...]
    act = silu_normed(hidden, g1_ref[...])
    for r in range(3):
        x1[r] = act[192 * r : 192 * r + 192]

    for i in range(3):
        for copy in copies2[i]:
            copy.wait()

        @pl.loop(0, C1 // 32)
        def _(n):
            rows = pl.ds(pl.multiple_of(32 * n, 32), 32)
            taps = {}
            for j, k in CORNERS:
                rp, u, b = corner_place(j, k)
                taps[j, k] = w2c[rp, b, u, i, rows, :].astype(F32)
            for m, (j, k) in enumerate(OTHERS):
                taps[j, k] = w2r[i, m, rows, :].astype(F32)
            for (rp, u, b), v in sums(taps).items():
                w2c[rp, b, u, i, rows, :] = v.astype(BF16)

    lhs = jnp.concatenate(
        [
            x1[u : u + 2, 32 * i : 32 * i + 128, :].reshape(256, C1)
            for u in range(2)
            for i in range(3)
        ],
        axis=1,
    )
    col = lax.broadcasted_iota(jnp.int32, (256, 1), 0) % W
    for rp in range(2):
        q0, qk, q2 = [
            jnp.dot(lhs, w2c[rp, b].reshape(6 * C1, C2), preferred_element_type=F32)
            for b in range(3)
        ]
        qk = qk + b2_ref[...]
        even = qk + jnp.where(col == 0, 0.0, pltpu.roll(q0, 1, 0) - q0)
        odd = qk + jnp.where(col == W - 1, 0.0, pltpu.roll(q2, 255, 0) - q2)
        for p, value in enumerate((even, odd)):
            act = silu_normed(value, g2_ref[...])
            for row in range(2):
                slot = 2 * row + 1 - rp
                for f in range(4):
                    part = act[128 * row + 32 * f : 128 * row + 32 * f + 32]
                    x2[slot, 64 * f + 32 * p : 64 * f + 32 * p + 32, :] = part

    for copy in copies3:
        copy.wait()

    @pl.loop(0, C2 // 32)
    def _(n):
        rows = pl.ds(pl.multiple_of(32 * n, 32), 32)
        for i in range(3):
            taps = {}
            for j, k in CORNERS:
                rp, u, b = corner_place(j, k)
                taps[j, k] = w3c[rp, u, i, rows, C3 * b : C3 * b + C3].astype(F32)
            for m, (j, k) in enumerate(OTHERS):
                taps[j, k] = w3r[i, m, rows, :].astype(F32)
            for (rp, u, b), v in sums(taps).items():
                w3c[rp, u, i, rows, C3 * b : C3 * b + C3] = v.astype(BF16)

    slots = [jnp.where(s == 0, 1, 0), 1, 2, jnp.where(s == SEQ - 1, 2, 3)]
    col = lax.broadcasted_iota(jnp.int32, (32, 1), 0)
    for rp in range(2):
        lhs = jnp.concatenate(
            [
                jnp.concatenate(
                    [x2[slots[rp + u + row], 64 * i : 64 * i + 128, :] for row in range(2)],
                    axis=0,
                )
                for u in range(2)
                for i in range(3)
            ],
            axis=1,
        )
        res = jnp.dot(lhs, w3c[rp].reshape(6 * C2, 3 * C3), preferred_element_type=F32)
        for row in range(2):
            for f in range(2):
                base = 128 * row + 64 * f
                (e0, ek, e2), (o0, ok, o2) = [
                    [
                        res[base + 32 * p : base + 32 * p + 32, C3 * b : C3 * b + C3]
                        for b in range(3)
                    ]
                    for p in range(2)
                ]
                ek = ek + b3_ref[...]
                ok = ok + b3_ref[...]
                values = (
                    ek + jnp.where(col == 0, 0.0, pltpu.roll(o0, 1, 0) - e0),
                    ek + (o2 - e2),
                    ok + (e0 - o0),
                    ok + jnp.where(col == W - 1, 0.0, pltpu.roll(e2, 31, 0) - o2),
                )
                for n, value in enumerate(values):
                    o32[f, 2 * row + rp, pl.ds(n, W, stride=4), :] = value
    out_ref[...] = o32[...].astype(BF16)


def decode(rows, w1, b1, g1, w2, b2, g2, w3, b3):
    vmem = pl.BlockSpec(memory_space=pltpu.VMEM)
    hbm = pl.BlockSpec(memory_space=pltpu.HBM)
    return pl.pallas_call(
        decode_kernel,
        out_shape=jax.ShapeDtypeStruct((2, 4, 128, C3), BF16),
        in_specs=[vmem, hbm, vmem, vmem, hbm, vmem, vmem, hbm, vmem],
        out_specs=vmem,
        scratch_shapes=[
            pltpu.VMEM((768, C1), BF16),
            pltpu.VMEM((2, 3, 2, 3, C1, C2), BF16),
            pltpu.VMEM((3, 5, C1, C2), BF16),
            pltpu.VMEM((2, 2, 3, C2, 3 * C3), BF16),
            pltpu.VMEM((3, 5, C2, C3), BF16),
            pltpu.VMEM((5, 8 * W, 128), F32),
            pltpu.VMEM((3, 6 * W, C1), BF16),
            pltpu.VMEM((4, 4 * 64, C2), BF16),
            pltpu.VMEM((2, 4, 128, C3), F32),
            pltpu.SemaphoreType.DMA((3, 3)),
            pltpu.SemaphoreType.DMA((3, 3, 3)),
            pltpu.SemaphoreType.DMA((3, 3, 3)),
        ],
        compiler_params=pltpu.CompilerParams(vmem_limit_bytes=56 << 20),
        name="decode",
    )(rows, w1, b1, g1, w2, b2, g2, w3, b3)


def per_device(latent, w1, b1, g1, w2, b2, g2, w3, b3):
    rows = gather_rows(latent)
    line = lambda v: v.reshape(1, -1)
    return decode(
        rows, w1.reshape(3, 3, 48, C1), line(b1), line(g1), w2, line(b2), line(g2), w3, line(b3)
    )


def solution(mesh):
    placed = (P(None, ("seq", "tm")), P(), P(), P(), P(), P(), P(), P(), P())
    return jax.shard_map(
        per_device,
        mesh=mesh,
        in_specs=placed,
        out_specs=P("tm", "seq", None, None),
        check_vma=False,
    )
```

```python
import jax
import jax.numpy as jnp
from jax import lax
from jax.experimental import pallas as pl
from jax.experimental.pallas import tpu as pltpu
from jax.sharding import PartitionSpec as P

MESH = pl.DeviceIdType.MESH
F32 = jnp.float32
BF16 = jnp.bfloat16

SEQ = 32
TM = 4
W = 32
C1, C2, C3 = 512, 256, 128
EPS = 1e-06

RAW = {(0, 0, 0): (0, 0), (0, 0, 2): (0, 2), (1, 1, 0): (2, 0), (1, 1, 2): (2, 2)}
SUMS = ((0, 0, 1), (0, 1, 0), (0, 1, 1), (0, 1, 2), (1, 0, 0), (1, 0, 1), (1, 0, 2), (1, 1, 1))
PEERS = tuple(
    (d, e) for d, e in (
        (2, 2), (-2, 2), (1, 2), (-1, 2), (2, 1), (2, 3), (-2, 1), (-2, 3), (0, 2), (1, 1), (1, 3),
        (-1, 1), (-1, 3), (2, 0), (-2, 0), (0, 1), (0, 3), (1, 0), (-1, 0),
    )
)


def silu_normed(hidden, gain):
    factor = lax.rsqrt(jnp.mean(hidden * hidden, axis=1, keepdims=True) + EPS)
    v = hidden * factor * gain
    half = 0.5 * v
    return (half + half * jnp.tanh(half)).astype(BF16)


def patches(lat_ref, pat_ref, s, t):
    late = 6 - 2 * t
    sub = lax.broadcasted_iota(jnp.int32, (8, 128), 0)
    lane = lax.broadcasted_iota(jnp.int32, (8, 128), 1)
    turned = []
    for q in range(5):
        row = jnp.clip(s - 2 + q, 0, SEQ - 1) - s + 2
        blocks = []
        for b in range(TM):
            x = lat_ref[row * TM + b].astype(F32)
            moved = pltpu.roll(x, late, 0)
            x = jnp.where(sub < late, jnp.broadcast_to(x[0:1], (8, 128)), moved)
            blocks.append([pltpu.roll(x, (128 - 16 * (m - 1)) % 128, 1) for m in range(8)])
        turned.append(blocks)

    def piece(q, c, up):
        b, m = c // 8, c % 8
        k = (m + 4) % 8 if up else m
        base = 64 if up else 0
        own = turned[q][b][k]
        if m == 0:
            other = turned[q][b - 1][k] if b else turned[q][0][(k + 1) % 8]
            own = jnp.where(lane < base + 16, other, own)
        if m == 7:
            other = turned[q][b + 1][k] if b < 3 else turned[q][3][(k + 7) % 8]
            own = jnp.where(lane >= base + 32, other, own)
        return own

    for q in range(5):
        for c in range(W):
            low = piece(q, c, False)
            if q < 4:
                high = jnp.where((lane >= 64) & (lane < 112), piece(q + 1, c, True), 0.0)
            else:
                high = jnp.zeros((8, 128), F32)
            pat_ref[q, pl.ds(c, 8, stride=W), :] = jnp.where(lane < 48, low, high)


def sums(taps):
    r12 = [taps[1, k] + taps[2, k] for k in range(3)]
    r01 = [taps[0, k] + taps[1, k] for k in range(3)]
    k0 = [taps[0, k] for k in range(3)]
    k2 = [taps[2, k] for k in range(3)]
    total = lambda r: r[0] + r[1] + r[2]
    return (total(k0), r12[0], total(r12), r12[2], r01[0], total(r01), r01[2], total(k2))


def add_taps(raw, summed, i, rows):
    taps = {(j, k): raw[i, j, k, rows, :].astype(F32) for j in range(3) for k in range(3)}
    for n, value in enumerate(sums(taps)):
        summed[i, n, rows, :] = value.astype(BF16)


def tap_matrix(raw, summed, rp, b):
    parts = []
    for u in range(2):
        for i in range(3):
            if (rp, u, b) in RAW:
                j, k = RAW[rp, u, b]
                parts.append(raw[i, j, k])
            else:
                parts.append(summed[i, SUMS.index((rp, u, b))])
    return jnp.concatenate(parts, axis=0)


def kernel(
    x_ref, w1_hbm, b1_ref, g1_ref, w2_hbm, b2_ref, g2_ref, w3_hbm, b3_ref,
    out_ref,
    lat, w1, w2, w2s, w3, w3s, pat, x1, x2, o32, send_sem, recv_sem, sem1, sem2, sem3,
):
    s, t = lax.axis_index("seq"), lax.axis_index("tm")

    def away(d, e):
        return (lax.rem(s + (d + SEQ), SEQ), lax.rem(t + e, TM))

    barrier = pltpu.get_barrier_semaphore()
    for d, e in PEERS:
        pl.semaphore_signal(barrier, inc=1, device_id=away(d, e), device_id_type=MESH)

    copies2 = [pltpu.make_async_copy(w2_hbm.at[i], w2.at[i], sem2.at[i]) for i in range(3)]
    copy1 = pltpu.make_async_copy(
        w1_hbm, w1.at[:, pl.ds(0, 3), pl.ds(0, 48), :], sem1
    )
    copy3 = pltpu.make_async_copy(w3_hbm, w3, sem3)
    for copy in copies2:
        copy.start()
    for i in range(3):
        w1[i, 3] = jnp.zeros((64, C1), BF16)
        for j in range(3):
            w1[i, j, 48:64, :] = jnp.zeros((16, C1), BF16)
    copy1.start()
    copy3.start()
    lat[2 * TM + t] = x_ref[...]

    pl.semaphore_wait(barrier, len(PEERS))
    for d, e in PEERS:
        pltpu.make_async_remote_copy(
            src_ref=x_ref,
            dst_ref=lat.at[(2 - d) * TM + t],
            send_sem=send_sem,
            recv_sem=recv_sem,
            device_id=away(d, e),
            device_id_type=MESH,
        ).start()

    for i in range(3):
        copies2[i].wait()

        @pl.loop(0, C1 // 32)
        def _(n):
            add_taps(w2, w2s, i, pl.ds(pl.multiple_of(32 * n, 32), 32))

    copy3.wait()

    @pl.loop(0, C2 // 32)
    def _(n):
        for i in range(3):
            add_taps(w3, w3s, i, pl.ds(pl.multiple_of(32 * n, 32), 32))

    copy1.wait()
    whole = lat.at[pl.ds(0, len(PEERS))]
    every = pltpu.make_async_remote_copy(
        src_ref=whole,
        dst_ref=whole,
        send_sem=send_sem,
        recv_sem=recv_sem,
        device_id=away(0, 1),
        device_id_type=MESH,
    )
    every.wait_recv()

    patches(lat, pat, s, t)
    lhs = []
    for r in range(3):
        q = jnp.clip(s - 1 + r, 0, SEQ - 1) - s + 1
        cols = []
        for i in range(3):
            for two in (0, 2):
                cols.append(pat[q + two, 32 * i : 32 * i + 192, :].astype(BF16))
        lhs.append(jnp.concatenate(cols, axis=1))
    lhs = jnp.concatenate(lhs, axis=0)
    hidden = jnp.dot(lhs, w1[...].reshape(768, C1), preferred_element_type=F32) + b1_ref[...]
    act = silu_normed(hidden, g1_ref[...])
    for r in range(3):
        x1[r] = act[192 * r : 192 * r + 192]

    lhs = jnp.concatenate(
        [
            x1[u : u + 2, 32 * i : 32 * i + 128, :].reshape(256, C1)
            for u in range(2)
            for i in range(3)
        ],
        axis=1,
    )
    col = lax.broadcasted_iota(jnp.int32, (256, 1), 0) % W
    for rp in range(2):
        q0, qk, q2 = [
            jnp.dot(lhs, tap_matrix(w2, w2s, rp, b), preferred_element_type=F32)
            for b in range(3)
        ]
        qk = qk + b2_ref[...]
        even = qk + jnp.where(col == 0, 0.0, pltpu.roll(q0, 1, 0) - q0)
        odd = qk + jnp.where(col == W - 1, 0.0, pltpu.roll(q2, 255, 0) - q2)
        for p, value in enumerate((even, odd)):
            act = silu_normed(value, g2_ref[...])
            for row in range(2):
                slot = 2 * row + 1 - rp
                for f in range(4):
                    part = act[128 * row + 32 * f : 128 * row + 32 * f + 32]
                    x2[slot, 64 * f + 32 * p : 64 * f + 32 * p + 32, :] = part

    slots = [jnp.where(s == 0, 1, 0), 1, 2, jnp.where(s == SEQ - 1, 2, 3)]
    col = lax.broadcasted_iota(jnp.int32, (32, 1), 0)
    for rp in range(2):
        lhs = jnp.concatenate(
            [
                jnp.concatenate(
                    [x2[slots[rp + u + row], 64 * i : 64 * i + 128, :] for row in range(2)],
                    axis=0,
                )
                for u in range(2)
                for i in range(3)
            ],
            axis=1,
        )
        rhs = jnp.concatenate([tap_matrix(w3, w3s, rp, b) for b in range(3)], axis=1)
        res = jnp.dot(lhs, rhs, preferred_element_type=F32)
        for row in range(2):
            for f in range(2):
                base = 128 * row + 64 * f
                (e0, ek, e2), (o0, ok, o2) = [
                    [
                        res[base + 32 * p : base + 32 * p + 32, C3 * b : C3 * b + C3]
                        for b in range(3)
                    ]
                    for p in range(2)
                ]
                ek = ek + b3_ref[...]
                ok = ok + b3_ref[...]
                values = (
                    ek + jnp.where(col == 0, 0.0, pltpu.roll(o0, 1, 0) - e0),
                    ek + (o2 - e2),
                    ok + (e0 - o0),
                    ok + jnp.where(col == W - 1, 0.0, pltpu.roll(e2, 31, 0) - o2),
                )
                for n, value in enumerate(values):
                    o32[f, 2 * row + rp, pl.ds(n, W, stride=4), :] = value
    out_ref[...] = o32[...].astype(BF16)

    every.wait_send()


def decode(x, w1, b1, g1, w2, b2, g2, w3, b3):
    vmem = pl.BlockSpec(memory_space=pltpu.VMEM)
    hbm = pl.BlockSpec(memory_space=pltpu.HBM)
    return pl.pallas_call(
        kernel,
        out_shape=jax.ShapeDtypeStruct((2, 4, 128, C3), BF16),
        in_specs=[vmem, hbm, vmem, vmem, hbm, vmem, vmem, hbm, vmem],
        out_specs=vmem,
        scratch_shapes=[
            pltpu.VMEM((5 * TM, 8, 128), BF16),
            pltpu.VMEM((3, 4, 64, C1), BF16),
            pltpu.VMEM((3, 3, 3, C1, C2), BF16),
            pltpu.VMEM((3, 8, C1, C2), BF16),
            pltpu.VMEM((3, 3, 3, C2, C3), BF16),
            pltpu.VMEM((3, 8, C2, C3), BF16),
            pltpu.VMEM((5, 8 * W, 128), F32),
            pltpu.VMEM((3, 6 * W, C1), BF16),
            pltpu.VMEM((4, 4 * 64, C2), BF16),
            pltpu.VMEM((2, 4, 128, C3), F32),
            pltpu.SemaphoreType.DMA,
            pltpu.SemaphoreType.DMA,
            pltpu.SemaphoreType.DMA,
            pltpu.SemaphoreType.DMA((3,)),
            pltpu.SemaphoreType.DMA,
        ],
        compiler_params=pltpu.CompilerParams(
            collective_id=0, has_side_effects=True, vmem_limit_bytes=56 << 20
        ),
        name="decode",
    )(x, w1, b1, g1, w2, b2, g2, w3, b3)


def per_device(latent, w1, b1, g1, w2, b2, g2, w3, b3):
    line = lambda v: v.reshape(1, -1)
    return decode(
        latent, w1.reshape(3, 3, 48, C1), line(b1), line(g1), w2, line(b2), line(g2), w3, line(b3)
    )


def solution(mesh):
    placed = (P(None, ("seq", "tm")), P(), P(), P(), P(), P(), P(), P(), P())
    return jax.shard_map(
        per_device,
        mesh=mesh,
        in_specs=placed,
        out_specs=P("tm", "seq", None, None),
        check_vma=False,
    )
```

```python
import jax
import jax.numpy as jnp
from jax import lax
from jax.experimental import pallas as pl
from jax.experimental.pallas import tpu as pltpu
from jax.sharding import PartitionSpec as P

MESH = pl.DeviceIdType.MESH
F32 = jnp.float32
BF16 = jnp.bfloat16

SEQ = 32
TM = 4
W = 32
C1, C2, C3 = 512, 256, 128
EPS = 1e-06

RAW = {(0, 0, 0): (0, 0), (0, 0, 2): (0, 2), (1, 1, 0): (2, 0), (1, 1, 2): (2, 2)}
SUMS = ((0, 0, 1), (0, 1, 0), (0, 1, 1), (0, 1, 2), (1, 0, 0), (1, 0, 1), (1, 0, 2), (1, 1, 1))
PEERS = tuple(
    (d, e) for d, e in (
        (2, 2), (-2, 2), (1, 2), (-1, 2), (2, 1), (2, 3), (-2, 1), (-2, 3), (0, 2), (1, 1), (1, 3),
        (-1, 1), (-1, 3), (2, 0), (-2, 0), (0, 1), (0, 3), (1, 0), (-1, 0),
    )
)


def silu_normed(hidden, gain):
    factor = lax.rsqrt(jnp.mean(hidden * hidden, axis=1, keepdims=True) + EPS)
    v = hidden * factor * gain
    half = 0.5 * v
    return (half + half * jnp.tanh(half)).astype(BF16)


def patches(lat_ref, pat_ref, s, t):
    late = 6 - 2 * t
    sub = lax.broadcasted_iota(jnp.int32, (8, 128), 0)
    lane = lax.broadcasted_iota(jnp.int32, (8, 128), 1)
    turned = []
    for q in range(5):
        row = jnp.clip(s - 2 + q, 0, SEQ - 1) - s + 2
        blocks = []
        for b in range(TM):
            x = lat_ref[row * TM + b].astype(F32)
            moved = pltpu.roll(x, late, 0)
            x = jnp.where(sub < late, jnp.broadcast_to(x[0:1], (8, 128)), moved)
            blocks.append([pltpu.roll(x, (128 - 16 * (m - 1)) % 128, 1) for m in range(8)])
        turned.append(blocks)

    def piece(q, c, up):
        b, m = c // 8, c % 8
        k = (m + 4) % 8 if up else m
        base = 64 if up else 0
        own = turned[q][b][k]
        if m == 0:
            other = turned[q][b - 1][k] if b else turned[q][0][(k + 1) % 8]
            own = jnp.where(lane < base + 16, other, own)
        if m == 7:
            other = turned[q][b + 1][k] if b < 3 else turned[q][3][(k + 7) % 8]
            own = jnp.where(lane >= base + 32, other, own)
        return own

    for q in range(5):
        for c in range(W):
            low = piece(q, c, False)
            if q < 4:
                high = jnp.where((lane >= 64) & (lane < 112), piece(q + 1, c, True), 0.0)
            else:
                high = jnp.zeros((8, 128), F32)
            pat_ref[q, pl.ds(c, 8, stride=W), :] = jnp.where(lane < 48, low, high)


def sums(taps):
    r12 = [taps[1, k] + taps[2, k] for k in range(3)]
    r01 = [taps[0, k] + taps[1, k] for k in range(3)]
    k0 = [taps[0, k] for k in range(3)]
    k2 = [taps[2, k] for k in range(3)]
    total = lambda r: r[0] + r[1] + r[2]
    return (total(k0), r12[0], total(r12), r12[2], r01[0], total(r01), r01[2], total(k2))


def add_taps(raw, summed, i, rows):
    taps = {(j, k): raw[i, j, k, rows, :].astype(F32) for j in range(3) for k in range(3)}
    for n, value in enumerate(sums(taps)):
        summed[i, n, rows, :] = value.astype(BF16)


def tap_matrix(raw, summed, rp, b):
    parts = []
    for u in range(2):
        for i in range(3):
            if (rp, u, b) in RAW:
                j, k = RAW[rp, u, b]
                parts.append(raw[i, j, k])
            else:
                parts.append(summed[i, SUMS.index((rp, u, b))])
    return jnp.concatenate(parts, axis=0)


def kernel(
    x_ref, w1_hbm, b1_ref, g1_ref, w2_hbm, b2_ref, g2_ref, w3_hbm, b3_ref,
    out_ref,
    lat, w1, w2, w2s, w3, w3s, pat, x1, x2, o32, send_sem, recv_sem, sem1, sem2, sem3,
):
    s, t = lax.axis_index("seq"), lax.axis_index("tm")

    def away(d, e):
        return (s + d, lax.rem(t + e, TM))

    def when_row(d):
        if d == 0:
            return lambda f: f()
        return pl.when(s + d >= 0 if d < 0 else s + d < SEQ)

    barrier = pltpu.get_barrier_semaphore()
    for d, e in PEERS:

        @when_row(d)
        def _():
            pl.semaphore_signal(barrier, inc=1, device_id=away(d, e), device_id_type=MESH)

    copies2 = [pltpu.make_async_copy(w2_hbm.at[i], w2.at[i], sem2.at[i]) for i in range(3)]
    copy1 = pltpu.make_async_copy(
        w1_hbm, w1.at[:, pl.ds(0, 3), pl.ds(0, 48), :], sem1
    )
    copy3 = pltpu.make_async_copy(w3_hbm, w3, sem3)
    for copy in copies2:
        copy.start()
    for i in range(3):
        w1[i, 3] = jnp.zeros((64, C1), BF16)
        for j in range(3):
            w1[i, j, 48:64, :] = jnp.zeros((16, C1), BF16)
    copy1.start()
    copy3.start()
    lat[2 * TM + t] = x_ref[...]

    rows = 1 + jnp.minimum(s, 2) + jnp.minimum(SEQ - 1 - s, 2)
    pl.semaphore_wait(barrier, TM * rows - 1)
    for d, e in PEERS:

        @when_row(d)
        def _():
            pltpu.make_async_remote_copy(
                src_ref=x_ref,
                dst_ref=lat.at[(2 - d) * TM + t],
                send_sem=send_sem.at[2 + d],
                recv_sem=recv_sem.at[2 - d],
                device_id=away(d, e),
                device_id_type=MESH,
            ).start()

    def all_of(d):
        some = lat.at[pl.ds(0, TM if d else TM - 1)]
        return pltpu.make_async_remote_copy(
            src_ref=some,
            dst_ref=some,
            send_sem=send_sem.at[2 + d],
            recv_sem=recv_sem.at[2 + d],
            device_id=away(0, 1),
            device_id_type=MESH,
        )

    for i in range(3):
        copies2[i].wait()

        @pl.loop(0, C1 // 32)
        def _(n):
            add_taps(w2, w2s, i, pl.ds(pl.multiple_of(32 * n, 32), 32))

    copy3.wait()

    @pl.loop(0, C2 // 32)
    def _(n):
        for i in range(3):
            add_taps(w3, w3s, i, pl.ds(pl.multiple_of(32 * n, 32), 32))

    copy1.wait()
    for d in (0, 1, -1, 2, -2):

        @when_row(d)
        def _():
            all_of(d).wait_recv()

    patches(lat, pat, s, t)
    lhs = []
    for r in range(3):
        q = jnp.clip(s - 1 + r, 0, SEQ - 1) - s + 1
        cols = []
        for i in range(3):
            for two in (0, 2):
                cols.append(pat[q + two, 32 * i : 32 * i + 192, :].astype(BF16))
        lhs.append(jnp.concatenate(cols, axis=1))
    lhs = jnp.concatenate(lhs, axis=0)
    hidden = jnp.dot(lhs, w1[...].reshape(768, C1), preferred_element_type=F32) + b1_ref[...]
    act = silu_normed(hidden, g1_ref[...])
    for r in range(3):
        x1[r] = act[192 * r : 192 * r + 192]

    lhs = jnp.concatenate(
        [
            x1[u : u + 2, 32 * i : 32 * i + 128, :].reshape(256, C1)
            for u in range(2)
            for i in range(3)
        ],
        axis=1,
    )
    col = lax.broadcasted_iota(jnp.int32, (256, 1), 0) % W
    for rp in range(2):
        q0, qk, q2 = [
            jnp.dot(lhs, tap_matrix(w2, w2s, rp, b), preferred_element_type=F32)
            for b in range(3)
        ]
        qk = qk + b2_ref[...]
        even = qk + jnp.where(col == 0, 0.0, pltpu.roll(q0, 1, 0) - q0)
        odd = qk + jnp.where(col == W - 1, 0.0, pltpu.roll(q2, 255, 0) - q2)
        for p, value in enumerate((even, odd)):
            act = silu_normed(value, g2_ref[...])
            for row in range(2):
                slot = 2 * row + 1 - rp
                for f in range(4):
                    part = act[128 * row + 32 * f : 128 * row + 32 * f + 32]
                    x2[slot, 64 * f + 32 * p : 64 * f + 32 * p + 32, :] = part

    slots = [jnp.where(s == 0, 1, 0), 1, 2, jnp.where(s == SEQ - 1, 2, 3)]
    col = lax.broadcasted_iota(jnp.int32, (32, 1), 0)
    for rp in range(2):
        lhs = jnp.concatenate(
            [
                jnp.concatenate(
                    [x2[slots[rp + u + row], 64 * i : 64 * i + 128, :] for row in range(2)],
                    axis=0,
                )
                for u in range(2)
                for i in range(3)
            ],
            axis=1,
        )
        rhs = jnp.concatenate([tap_matrix(w3, w3s, rp, b) for b in range(3)], axis=1)
        res = jnp.dot(lhs, rhs, preferred_element_type=F32)
        for row in range(2):
            for f in range(2):
                base = 128 * row + 64 * f
                (e0, ek, e2), (o0, ok, o2) = [
                    [
                        res[base + 32 * p : base + 32 * p + 32, C3 * b : C3 * b + C3]
                        for b in range(3)
                    ]
                    for p in range(2)
                ]
                ek = ek + b3_ref[...]
                ok = ok + b3_ref[...]
                values = (
                    ek + jnp.where(col == 0, 0.0, pltpu.roll(o0, 1, 0) - e0),
                    ek + (o2 - e2),
                    ok + (e0 - o0),
                    ok + jnp.where(col == W - 1, 0.0, pltpu.roll(e2, 31, 0) - o2),
                )
                for n, value in enumerate(values):
                    o32[f, 2 * row + rp, pl.ds(n, W, stride=4), :] = value
    out_ref[...] = o32[...].astype(BF16)

    for d in (0, 1, -1, 2, -2):

        @when_row(d)
        def _():
            all_of(d).wait_send()


def decode(x, w1, b1, g1, w2, b2, g2, w3, b3):
    vmem = pl.BlockSpec(memory_space=pltpu.VMEM)
    hbm = pl.BlockSpec(memory_space=pltpu.HBM)
    return pl.pallas_call(
        kernel,
        out_shape=jax.ShapeDtypeStruct((2, 4, 128, C3), BF16),
        in_specs=[vmem, hbm, vmem, vmem, hbm, vmem, vmem, hbm, vmem],
        out_specs=vmem,
        scratch_shapes=[
            pltpu.VMEM((5 * TM, 8, 128), BF16),
            pltpu.VMEM((3, 4, 64, C1), BF16),
            pltpu.VMEM((3, 3, 3, C1, C2), BF16),
            pltpu.VMEM((3, 8, C1, C2), BF16),
            pltpu.VMEM((3, 3, 3, C2, C3), BF16),
            pltpu.VMEM((3, 8, C2, C3), BF16),
            pltpu.VMEM((5, 8 * W, 128), F32),
            pltpu.VMEM((3, 6 * W, C1), BF16),
            pltpu.VMEM((4, 4 * 64, C2), BF16),
            pltpu.VMEM((2, 4, 128, C3), F32),
            pltpu.SemaphoreType.DMA((5,)),
            pltpu.SemaphoreType.DMA((5,)),
            pltpu.SemaphoreType.DMA,
            pltpu.SemaphoreType.DMA((3,)),
            pltpu.SemaphoreType.DMA,
        ],
        compiler_params=pltpu.CompilerParams(
            collective_id=0, has_side_effects=True, vmem_limit_bytes=56 << 20
        ),
        name="decode",
    )(x, w1, b1, g1, w2, b2, g2, w3, b3)


def per_device(latent, w1, b1, g1, w2, b2, g2, w3, b3):
    line = lambda v: v.reshape(1, -1)
    return decode(
        latent, w1.reshape(3, 3, 48, C1), line(b1), line(g1), w2, line(b2), line(g2), w3, line(b3)
    )


def solution(mesh):
    placed = (P(None, ("seq", "tm")), P(), P(), P(), P(), P(), P(), P(), P())
    return jax.shard_map(
        per_device,
        mesh=mesh,
        in_specs=placed,
        out_specs=P("tm", "seq", None, None),
        check_vma=False,
    )
```

```python
import jax
import jax.numpy as jnp
from jax import lax
from jax.experimental import pallas as pl
from jax.experimental.pallas import tpu as pltpu
from jax.sharding import PartitionSpec as P

MESH = pl.DeviceIdType.MESH
F32 = jnp.float32
BF16 = jnp.bfloat16

SEQ = 32
TM = 4
W = 32
C1, C2, C3 = 512, 256, 128
EPS = 1e-06

RAW = {(0, 0, 0): (0, 0), (0, 0, 2): (0, 2), (1, 1, 0): (2, 0), (1, 1, 2): (2, 2)}
SUMS = ((0, 0, 1), (0, 1, 0), (0, 1, 1), (0, 1, 2), (1, 0, 0), (1, 0, 1), (1, 0, 2), (1, 1, 1))
PEERS = tuple(
    (d, e) for d, e in (
        (2, 2), (-2, 2), (1, 2), (-1, 2), (2, 1), (2, 3), (-2, 1), (-2, 3), (0, 2), (1, 1), (1, 3),
        (-1, 1), (-1, 3), (2, 0), (-2, 0), (0, 1), (0, 3), (1, 0), (-1, 0),
    )
)


def silu_normed(hidden, gain):
    factor = lax.rsqrt(jnp.mean(hidden * hidden, axis=1, keepdims=True) + EPS)
    v = hidden * factor * gain
    half = 0.5 * v
    return (half + half * jnp.tanh(half)).astype(BF16)


def patches(lat_ref, pat_ref, s, t):
    late = 6 - 2 * t
    sub = lax.broadcasted_iota(jnp.int32, (8, 128), 0)
    lane = lax.broadcasted_iota(jnp.int32, (8, 128), 1)
    turned = []
    for q in range(5):
        row = jnp.clip(s - 2 + q, 0, SEQ - 1) - s + 2
        blocks = []
        for b in range(TM):
            x = lat_ref[row * TM + b].astype(F32)
            moved = pltpu.roll(x, late, 0)
            x = jnp.where(sub < late, jnp.broadcast_to(x[0:1], (8, 128)), moved)
            blocks.append([pltpu.roll(x, (128 - 16 * (m - 1)) % 128, 1) for m in range(8)])
        turned.append(blocks)

    def piece(q, c, up):
        b, m = c // 8, c % 8
        k = (m + 4) % 8 if up else m
        base = 64 if up else 0
        own = turned[q][b][k]
        if m == 0:
            other = turned[q][b - 1][k] if b else turned[q][0][(k + 1) % 8]
            own = jnp.where(lane < base + 16, other, own)
        if m == 7:
            other = turned[q][b + 1][k] if b < 3 else turned[q][3][(k + 7) % 8]
            own = jnp.where(lane >= base + 32, other, own)
        return own

    for q in range(5):
        for c in range(W):
            low = piece(q, c, False)
            if q < 4:
                high = jnp.where((lane >= 64) & (lane < 112), piece(q + 1, c, True), 0.0)
            else:
                high = jnp.zeros((8, 128), F32)
            pat_ref[q, pl.ds(c, 8, stride=W), :] = jnp.where(lane < 48, low, high)


def sums(taps):
    r12 = [taps[1, k] + taps[2, k] for k in range(3)]
    r01 = [taps[0, k] + taps[1, k] for k in range(3)]
    k0 = [taps[0, k] for k in range(3)]
    k2 = [taps[2, k] for k in range(3)]
    total = lambda r: r[0] + r[1] + r[2]
    return (total(k0), r12[0], total(r12), r12[2], r01[0], total(r01), r01[2], total(k2))


def add_taps(raw, summed, i, rows):
    taps = {(j, k): raw[i, j, k, rows, :].astype(F32) for j in range(3) for k in range(3)}
    for n, value in enumerate(sums(taps)):
        summed[i, n, rows, :] = value.astype(BF16)


def tap_matrix(raw, summed, rp, b):
    parts = []
    for u in range(2):
        for i in range(3):
            if (rp, u, b) in RAW:
                j, k = RAW[rp, u, b]
                parts.append(raw[i, j, k])
            else:
                parts.append(summed[i, SUMS.index((rp, u, b))])
    return jnp.concatenate(parts, axis=0)


def gather_kernel(
    x_ref, w1_hbm, w2_hbm, w3_hbm,
    lat, w1, w2, w2s, w3, w3s,
    send_sem, recv_sem, sem1, sem2, sem3,
):
    s, t = lax.axis_index("seq"), lax.axis_index("tm")

    def away(d, e):
        return (s + d, lax.rem(t + e, TM))

    def when_row(d):
        if d == 0:
            return lambda f: f()
        return pl.when(s + d >= 0 if d < 0 else s + d < SEQ)

    barrier = pltpu.get_barrier_semaphore()
    for d, e in PEERS:

        @when_row(d)
        def _():
            pl.semaphore_signal(barrier, inc=1, device_id=away(d, e), device_id_type=MESH)

    copies2 = [pltpu.make_async_copy(w2_hbm.at[i], w2.at[i], sem2.at[i]) for i in range(3)]
    copy1 = pltpu.make_async_copy(
        w1_hbm, w1.at[:, pl.ds(0, 3), pl.ds(0, 48), :], sem1
    )
    copy3 = pltpu.make_async_copy(w3_hbm, w3, sem3)
    for copy in copies2:
        copy.start()
    for i in range(3):
        w1[i, 3] = jnp.zeros((64, C1), BF16)
        for j in range(3):
            w1[i, j, 48:64, :] = jnp.zeros((16, C1), BF16)
    copy1.start()
    copy3.start()
    lat[2 * TM + t] = x_ref[...]

    rows = 1 + jnp.minimum(s, 2) + jnp.minimum(SEQ - 1 - s, 2)
    pl.semaphore_wait(barrier, TM * rows - 1)
    for d, e in PEERS:

        @when_row(d)
        def _():
            pltpu.make_async_remote_copy(
                src_ref=x_ref,
                dst_ref=lat.at[(2 - d) * TM + t],
                send_sem=send_sem.at[2 + d],
                recv_sem=recv_sem.at[2 - d],
                device_id=away(d, e),
                device_id_type=MESH,
            ).start()

    def all_of(d):
        some = lat.at[pl.ds(0, TM if d else TM - 1)]
        return pltpu.make_async_remote_copy(
            src_ref=some,
            dst_ref=some,
            send_sem=send_sem.at[2 + d],
            recv_sem=recv_sem.at[2 + d],
            device_id=away(0, 1),
            device_id_type=MESH,
        )

    for i in range(3):
        copies2[i].wait()

        @pl.loop(0, C1 // 32)
        def _(n):
            add_taps(w2, w2s, i, pl.ds(pl.multiple_of(32 * n, 32), 32))

    copy3.wait()

    @pl.loop(0, C2 // 32)
    def _(n):
        for i in range(3):
            add_taps(w3, w3s, i, pl.ds(pl.multiple_of(32 * n, 32), 32))

    copy1.wait()
    for d in (0, 1, -1, 2, -2):

        @when_row(d)
        def _():
            all_of(d).wait_recv()

    for d in (0, 1, -1, 2, -2):

        @when_row(d)
        def _():
            all_of(d).wait_send()


def decode_kernel(
    lat, w1, w2, w2s, w3, w3s, b1_ref, g1_ref, b2_ref, g2_ref, b3_ref,
    out_ref,
    pat, x1, x2, o32,
):
    s, t = lax.axis_index("seq"), lax.axis_index("tm")

    patches(lat, pat, s, t)
    lhs = []
    for r in range(3):
        q = jnp.clip(s - 1 + r, 0, SEQ - 1) - s + 1
        cols = []
        for i in range(3):
            for two in (0, 2):
                cols.append(pat[q + two, 32 * i : 32 * i + 192, :].astype(BF16))
        lhs.append(jnp.concatenate(cols, axis=1))
    lhs = jnp.concatenate(lhs, axis=0)
    hidden = jnp.dot(lhs, w1[...].reshape(768, C1), preferred_element_type=F32) + b1_ref[...]
    act = silu_normed(hidden, g1_ref[...])
    for r in range(3):
        x1[r] = act[192 * r : 192 * r + 192]

    lhs = jnp.concatenate(
        [
            x1[u : u + 2, 32 * i : 32 * i + 128, :].reshape(256, C1)
            for u in range(2)
            for i in range(3)
        ],
        axis=1,
    )
    col = lax.broadcasted_iota(jnp.int32, (256, 1), 0) % W
    for rp in range(2):
        q0, qk, q2 = [
            jnp.dot(lhs, tap_matrix(w2, w2s, rp, b), preferred_element_type=F32)
            for b in range(3)
        ]
        qk = qk + b2_ref[...]
        even = qk + jnp.where(col == 0, 0.0, pltpu.roll(q0, 1, 0) - q0)
        odd = qk + jnp.where(col == W - 1, 0.0, pltpu.roll(q2, 255, 0) - q2)
        for p, value in enumerate((even, odd)):
            act = silu_normed(value, g2_ref[...])
            for row in range(2):
                slot = 2 * row + 1 - rp
                for f in range(4):
                    part = act[128 * row + 32 * f : 128 * row + 32 * f + 32]
                    x2[slot, 64 * f + 32 * p : 64 * f + 32 * p + 32, :] = part

    slots = [jnp.where(s == 0, 1, 0), 1, 2, jnp.where(s == SEQ - 1, 2, 3)]
    col = lax.broadcasted_iota(jnp.int32, (32, 1), 0)
    for rp in range(2):
        lhs = jnp.concatenate(
            [
                jnp.concatenate(
                    [x2[slots[rp + u + row], 64 * i : 64 * i + 128, :] for row in range(2)],
                    axis=0,
                )
                for u in range(2)
                for i in range(3)
            ],
            axis=1,
        )
        rhs = jnp.concatenate([tap_matrix(w3, w3s, rp, b) for b in range(3)], axis=1)
        res = jnp.dot(lhs, rhs, preferred_element_type=F32)
        for row in range(2):
            for f in range(2):
                base = 128 * row + 64 * f
                (e0, ek, e2), (o0, ok, o2) = [
                    [
                        res[base + 32 * p : base + 32 * p + 32, C3 * b : C3 * b + C3]
                        for b in range(3)
                    ]
                    for p in range(2)
                ]
                ek = ek + b3_ref[...]
                ok = ok + b3_ref[...]
                values = (
                    ek + jnp.where(col == 0, 0.0, pltpu.roll(o0, 1, 0) - e0),
                    ek + (o2 - e2),
                    ok + (e0 - o0),
                    ok + jnp.where(col == W - 1, 0.0, pltpu.roll(e2, 31, 0) - o2),
                )
                for n, value in enumerate(values):
                    o32[f, 2 * row + rp, pl.ds(n, W, stride=4), :] = value
    out_ref[...] = o32[...].astype(BF16)


def per_device(latent, w1, b1, g1, w2, b2, g2, w3, b3):
    line = lambda v: v.reshape(1, -1)
    vmem = pl.BlockSpec(memory_space=pltpu.VMEM)
    hbm = pl.BlockSpec(memory_space=pltpu.HBM)
    in_hbm = lambda v: pltpu.with_memory_space_constraint(v, pltpu.HBM)
    kept = pl.pallas_call(
        gather_kernel,
        out_shape=[
            pltpu.VMEM((5 * TM, 8, 128), BF16),
            pltpu.VMEM((3, 4, 64, C1), BF16),
            pltpu.VMEM((3, 3, 3, C1, C2), BF16),
            pltpu.VMEM((3, 8, C1, C2), BF16),
            pltpu.VMEM((3, 3, 3, C2, C3), BF16),
            pltpu.VMEM((3, 8, C2, C3), BF16),
        ],
        in_specs=[vmem, hbm, hbm, hbm],
        out_specs=[vmem] * 6,
        scratch_shapes=[
            pltpu.SemaphoreType.DMA((5,)),
            pltpu.SemaphoreType.DMA((5,)),
            pltpu.SemaphoreType.DMA,
            pltpu.SemaphoreType.DMA((3,)),
            pltpu.SemaphoreType.DMA,
        ],
        compiler_params=pltpu.CompilerParams(
            collective_id=0, has_side_effects=True, vmem_limit_bytes=8 << 20
        ),
        name="gather",
    )(*map(in_hbm, (latent, w1.reshape(3, 3, 48, C1), w2, w3)))
    return pl.pallas_call(
        decode_kernel,
        out_shape=jax.ShapeDtypeStruct((2, 4, 128, C3), BF16),
        in_specs=[vmem] * 11,
        out_specs=vmem,
        scratch_shapes=[
            pltpu.VMEM((5, 8 * W, 128), F32),
            pltpu.VMEM((3, 6 * W, C1), BF16),
            pltpu.VMEM((4, 4 * 64, C2), BF16),
            pltpu.VMEM((2, 4, 128, C3), F32),
        ],
        compiler_params=pltpu.CompilerParams(vmem_limit_bytes=24 << 20),
        name="decode",
    )(*kept, line(b1), line(g1), line(b2), line(g2), line(b3))


def solution(mesh):
    placed = (P(None, ("seq", "tm")), P(), P(), P(), P(), P(), P(), P(), P())
    return jax.shard_map(
        per_device,
        mesh=mesh,
        in_specs=placed,
        out_specs=P("tm", "seq", None, None),
        check_vma=False,
    )
```

```python
import jax
import jax.numpy as jnp
from jax import lax
from jax.experimental import pallas as pl
from jax.experimental.pallas import tpu as pltpu
from jax.sharding import PartitionSpec as P

MESH = pl.DeviceIdType.MESH
F32 = jnp.float32
BF16 = jnp.bfloat16

SEQ = 32
TM = 4
W = 32
C1, C2, C3 = 512, 256, 128
EPS = 1e-06

RAW = {(0, 0, 0): (0, 0), (0, 0, 2): (0, 2), (1, 1, 0): (2, 0), (1, 1, 2): (2, 2)}
SUMS = ((0, 0, 1), (0, 1, 0), (0, 1, 1), (0, 1, 2), (1, 0, 0), (1, 0, 1), (1, 0, 2), (1, 1, 1))
PEERS = tuple(
    (d, e) for d, e in (
        (2, 2), (-2, 2), (1, 2), (-1, 2), (2, 1), (2, 3), (-2, 1), (-2, 3), (0, 2), (1, 1), (1, 3),
        (-1, 1), (-1, 3), (2, 0), (-2, 0), (0, 1), (0, 3), (1, 0), (-1, 0),
    )
)


def silu_normed(hidden, gain):
    factor = lax.rsqrt(jnp.mean(hidden * hidden, axis=1, keepdims=True) + EPS)
    v = hidden * factor * gain
    half = 0.5 * v
    return (half + half * jnp.tanh(half)).astype(BF16)


def patches(lat_ref, pat_ref, s, t):
    late = 6 - 2 * t
    sub = lax.broadcasted_iota(jnp.int32, (8, 128), 0)
    lane = lax.broadcasted_iota(jnp.int32, (8, 128), 1)
    turned = []
    for q in range(5):
        row = jnp.clip(s - 2 + q, 0, SEQ - 1) - s + 2
        blocks = []
        for b in range(TM):
            x = lat_ref[row * TM + b].astype(F32)
            moved = pltpu.roll(x, late, 0)
            x = jnp.where(sub < late, jnp.broadcast_to(x[0:1], (8, 128)), moved)
            blocks.append([pltpu.roll(x, (128 - 16 * (m - 1)) % 128, 1) for m in range(8)])
        turned.append(blocks)

    def piece(q, c, up):
        b, m = c // 8, c % 8
        k = (m + 4) % 8 if up else m
        base = 64 if up else 0
        own = turned[q][b][k]
        if m == 0:
            other = turned[q][b - 1][k] if b else turned[q][0][(k + 1) % 8]
            own = jnp.where(lane < base + 16, other, own)
        if m == 7:
            other = turned[q][b + 1][k] if b < 3 else turned[q][3][(k + 7) % 8]
            own = jnp.where(lane >= base + 32, other, own)
        return own

    for q in range(5):
        for c in range(W):
            low = piece(q, c, False)
            if q < 4:
                high = jnp.where((lane >= 64) & (lane < 112), piece(q + 1, c, True), 0.0)
            else:
                high = jnp.zeros((8, 128), F32)
            pat_ref[q, pl.ds(c, 8, stride=W), :] = jnp.where(lane < 48, low, high)


def add_taps(raw, summed, i, rows):
    taps = {(j, k): raw[i, j, k, rows, :] for j in range(3) for k in range(3)}
    wide = {place: value.astype(F32) for place, value in taps.items()}
    total = [wide[j, 0] + wide[j, 1] + wide[j, 2] for j in range(3)]
    values = (
        total[0],
        taps[1, 0] + taps[2, 0],
        total[1] + total[2],
        taps[1, 2] + taps[2, 2],
        taps[0, 0] + taps[1, 0],
        total[0] + total[1],
        taps[0, 2] + taps[1, 2],
        total[2],
    )
    for n, value in enumerate(values):
        summed[i, n, rows, :] = value.astype(BF16)


def tap_matrix(raw, summed, rp, b):
    parts = []
    for u in range(2):
        for i in range(3):
            if (rp, u, b) in RAW:
                j, k = RAW[rp, u, b]
                parts.append(raw[i, j, k])
            else:
                parts.append(summed[i, SUMS.index((rp, u, b))])
    return jnp.concatenate(parts, axis=0)


def gather_kernel(
    x_hbm, w1_hbm, w2_hbm, w3_hbm,
    lat, w1, w2, w2s, w3, w3s,
    send_sem, recv_sem, own_sem, sem1, sem2, sem3,
):
    s, t = lax.axis_index("seq"), lax.axis_index("tm")

    def away(d, e):
        return (s + d, lax.rem(t + e, TM))

    def when_row(d):
        if d == 0:
            return lambda f: f()
        return pl.when(s + d >= 0 if d < 0 else s + d < SEQ)

    barrier = pltpu.get_barrier_semaphore()
    for d, e in PEERS:

        @when_row(d)
        def _():
            pl.semaphore_signal(barrier, inc=1, device_id=away(d, e), device_id_type=MESH)

    own = lat.at[2 * TM + t]
    own_copy = pltpu.make_async_copy(x_hbm, own, own_sem)
    own_copy.start()

    copies2 = [pltpu.make_async_copy(w2_hbm.at[i], w2.at[i], sem2.at[i]) for i in range(3)]
    copy1 = pltpu.make_async_copy(
        w1_hbm, w1.at[:, pl.ds(0, 3), pl.ds(0, 48), :], sem1
    )
    copy3 = pltpu.make_async_copy(w3_hbm, w3, sem3)
    for copy in copies2:
        copy.start(priority=1)
    for i in range(3):
        w1[i, 3] = jnp.zeros((64, C1), BF16)
        for j in range(3):
            w1[i, j, 48:64, :] = jnp.zeros((16, C1), BF16)
    copy1.start(priority=1)
    copy3.start(priority=1)

    rows = 1 + jnp.minimum(s, 2) + jnp.minimum(SEQ - 1 - s, 2)
    own_copy.wait()
    pl.semaphore_wait(barrier, TM * rows - 1)
    for d, e in PEERS:

        @when_row(d)
        def _():
            pltpu.make_async_remote_copy(
                src_ref=own,
                dst_ref=lat.at[(2 - d) * TM + t],
                send_sem=send_sem.at[2 + d],
                recv_sem=recv_sem.at[2 - d],
                device_id=away(d, e),
                device_id_type=MESH,
            ).start()

    def all_of(d):
        some = lat.at[pl.ds(0, TM if d else TM - 1)]
        return pltpu.make_async_remote_copy(
            src_ref=some,
            dst_ref=some,
            send_sem=send_sem.at[2 + d],
            recv_sem=recv_sem.at[2 + d],
            device_id=away(0, 1),
            device_id_type=MESH,
        )

    for i in range(3):
        copies2[i].wait()

        @pl.loop(0, C1 // 64)
        def _(n):
            add_taps(w2, w2s, i, pl.ds(pl.multiple_of(64 * n, 64), 64))

    copy3.wait()

    @pl.loop(0, C2 // 32)
    def _(n):
        for i in range(3):
            add_taps(w3, w3s, i, pl.ds(pl.multiple_of(32 * n, 32), 32))

    copy1.wait()
    for d in (0, 1, -1, 2, -2):

        @when_row(d)
        def _():
            all_of(d).wait_recv()

    for d in (0, 1, -1, 2, -2):

        @when_row(d)
        def _():
            all_of(d).wait_send()


def convolutions(s, pat, w1, w2, w2s, b1_ref, g1_ref, b2_ref, g2_ref, x1, x2, first):
    start = 4 if first else 0
    size = W * (6 - start)
    lhs = []
    for r in range(3):
        q = jnp.clip(s - 1 + r, 0, SEQ - 1) - s + 1
        cols = []
        for i in range(3):
            for two in (0, 2):
                at = W * (i + start)
                cols.append(pat[q + two, at : at + size, :].astype(BF16))
        lhs.append(jnp.concatenate(cols, axis=1))
    lhs = jnp.concatenate(lhs, axis=0)
    hidden = jnp.dot(lhs, w1[...].reshape(768, C1), preferred_element_type=F32) + b1_ref[...]
    act = silu_normed(hidden, g1_ref[...])
    for r in range(3):
        x1[r, W * start : W * 6, :] = act[size * r : size * r + size]
        for k in range(first, start):
            x1[r, W * k : W * k + W, :] = act[size * r : size * r + W]

    frames = 4 - first
    size = W * frames
    lhs = jnp.concatenate(
        [
            x1[u : u + 2, W * (i + first) : W * (i + first) + size, :].reshape(2 * size, C1)
            for u in range(2)
            for i in range(3)
        ],
        axis=1,
    )
    col = lax.broadcasted_iota(jnp.int32, (2 * size, 1), 0) % W
    for rp in range(2):
        q0, qk, q2 = [
            jnp.dot(lhs, tap_matrix(w2, w2s, rp, b), preferred_element_type=F32)
            for b in range(3)
        ]
        qk = qk + b2_ref[...]
        even = qk + jnp.where(col == 0, 0.0, pltpu.roll(q0, 1, 0) - q0)
        odd = qk + jnp.where(col == W - 1, 0.0, pltpu.roll(q2, 2 * size - 1, 0) - q2)
        for p, value in enumerate((even, odd)):
            act = silu_normed(value, g2_ref[...])
            for row in range(2):
                slot = 2 * row + 1 - rp
                for f in range(frames):
                    part = act[size * row + W * f : size * row + W * f + W]
                    at = 64 * (f + first) + W * p
                    x2[slot, at : at + W, :] = part


def decode_kernel(
    lat, w1, w2, w2s, w3, w3s, b1_ref, g1_ref, b2_ref, g2_ref, b3_ref,
    out_ref,
    pat, x1, x2, o32,
):
    s, t = lax.axis_index("seq"), lax.axis_index("tm")

    patches(lat, pat, s, t)

    @pl.when(t == 0)
    def _():
        convolutions(s, pat, w1, w2, w2s, b1_ref, g1_ref, b2_ref, g2_ref, x1, x2, 2)
        for slot in range(4):
            third = x2[slot, 128:192, :]
            x2[slot, 0:64, :] = third
            x2[slot, 64:128, :] = third

    @pl.when(t > 0)
    def _():
        convolutions(s, pat, w1, w2, w2s, b1_ref, g1_ref, b2_ref, g2_ref, x1, x2, 0)

    slots = [jnp.where(s == 0, 1, 0), 1, 2, jnp.where(s == SEQ - 1, 2, 3)]
    col = lax.broadcasted_iota(jnp.int32, (32, 1), 0)
    for rp in range(2):
        lhs = jnp.concatenate(
            [
                jnp.concatenate(
                    [x2[slots[rp + u + row], 64 * i : 64 * i + 128, :] for row in range(2)],
                    axis=0,
                )
                for u in range(2)
                for i in range(3)
            ],
            axis=1,
        )
        rhs = jnp.concatenate([tap_matrix(w3, w3s, rp, b) for b in range(3)], axis=1)
        res = jnp.dot(lhs, rhs, preferred_element_type=F32)
        for row in range(2):
            for f in range(2):
                base = 128 * row + 64 * f
                (e0, ek, e2), (o0, ok, o2) = [
                    [
                        res[base + 32 * p : base + 32 * p + 32, C3 * b : C3 * b + C3]
                        for b in range(3)
                    ]
                    for p in range(2)
                ]
                ek = ek + b3_ref[...]
                ok = ok + b3_ref[...]
                values = (
                    ek + jnp.where(col == 0, 0.0, pltpu.roll(o0, 1, 0) - e0),
                    ek + (o2 - e2),
                    ok + (e0 - o0),
                    ok + jnp.where(col == W - 1, 0.0, pltpu.roll(e2, 31, 0) - o2),
                )
                for n, value in enumerate(values):
                    o32[f, 2 * row + rp, pl.ds(n, W, stride=4), :] = value
    out_ref[...] = o32[...].astype(BF16)


def per_device(latent, w1, b1, g1, w2, b2, g2, w3, b3):
    line = lambda v: v.reshape(1, -1)
    vmem = pl.BlockSpec(memory_space=pltpu.VMEM)
    hbm = pl.BlockSpec(memory_space=pltpu.HBM)
    in_hbm = lambda v: pltpu.with_memory_space_constraint(v, pltpu.HBM)
    kept = pl.pallas_call(
        gather_kernel,
        out_shape=[
            pltpu.VMEM((5 * TM, 8, 128), BF16),
            pltpu.VMEM((3, 4, 64, C1), BF16),
            pltpu.VMEM((3, 3, 3, C1, C2), BF16),
            pltpu.VMEM((3, 8, C1, C2), BF16),
            pltpu.VMEM((3, 3, 3, C2, C3), BF16),
            pltpu.VMEM((3, 8, C2, C3), BF16),
        ],
        in_specs=[hbm] * 4,
        out_specs=[vmem] * 6,
        scratch_shapes=[
            pltpu.SemaphoreType.DMA((5,)),
            pltpu.SemaphoreType.DMA((5,)),
            pltpu.SemaphoreType.DMA,
            pltpu.SemaphoreType.DMA,
            pltpu.SemaphoreType.DMA((3,)),
            pltpu.SemaphoreType.DMA,
        ],
        compiler_params=pltpu.CompilerParams(
            collective_id=0, has_side_effects=True, vmem_limit_bytes=8 << 20
        ),
        name="gather",
    )(*map(in_hbm, (latent, w1.reshape(3, 3, 48, C1), w2, w3)))
    return pl.pallas_call(
        decode_kernel,
        out_shape=jax.ShapeDtypeStruct((2, 4, 128, C3), BF16),
        in_specs=[vmem] * 11,
        out_specs=vmem,
        scratch_shapes=[
            pltpu.VMEM((5, 8 * W, 128), F32),
            pltpu.VMEM((3, 6 * W, C1), BF16),
            pltpu.VMEM((4, 4 * 64, C2), BF16),
            pltpu.VMEM((2, 4, 128, C3), F32),
        ],
        compiler_params=pltpu.CompilerParams(vmem_limit_bytes=24 << 20),
        name="decode",
    )(*kept, line(b1), line(g1), line(b2), line(g2), line(b3))


def solution(mesh):
    placed = (P(None, ("seq", "tm")), P(), P(), P(), P(), P(), P(), P(), P())
    return jax.shard_map(
        per_device,
        mesh=mesh,
        in_specs=placed,
        out_specs=P("tm", "seq", None, None),
        check_vma=False,
    )
```

```python
import jax
import jax.numpy as jnp
from jax import lax
from jax.experimental import pallas as pl
from jax.experimental.pallas import tpu as pltpu
from jax.sharding import PartitionSpec as P

MESH = pl.DeviceIdType.MESH
F32 = jnp.float32
BF16 = jnp.bfloat16

SEQ = 32
TM = 4
W = 32
CHUNK = 16
C1, C2, C3 = 512, 256, 128
EPS = 1e-06

RAW = {(0, 0, 0): (0, 0), (0, 0, 2): (0, 2), (1, 1, 0): (2, 0), (1, 1, 2): (2, 2)}
SUMS = ((0, 0, 1), (0, 1, 0), (0, 1, 1), (0, 1, 2), (1, 0, 0), (1, 0, 1), (1, 0, 2), (1, 1, 1))
PLACES = SUMS + tuple(RAW)
KEPT = tuple((n, p) for n in range(4) for p in (SUMS if n in (0, 3) else PLACES))
PEERS = tuple(
    (d, e) for d, e in (
        (2, 2), (-2, 2), (1, 2), (-1, 2), (2, 1), (2, 3), (-2, 1), (-2, 3), (0, 2), (1, 1), (1, 3),
        (-1, 1), (-1, 3), (2, 0), (-2, 0), (0, 1), (0, 3), (1, 0), (-1, 0),
    )
)


def silu_normed(hidden, gain):
    factor = lax.rsqrt(jnp.mean(hidden * hidden, axis=1, keepdims=True) + EPS)
    v = hidden * factor * gain
    half = 0.5 * v
    return (half + half * jnp.tanh(half)).astype(BF16)


def patches(lat_ref, pat_ref, s, t):
    late = 6 - 2 * t
    sub = lax.broadcasted_iota(jnp.int32, (8, 128), 0)
    lane = lax.broadcasted_iota(jnp.int32, (8, 128), 1)
    turned = []
    for q in range(5):
        row = jnp.clip(s - 2 + q, 0, SEQ - 1) - s + 2
        blocks = []
        for b in range(TM):
            x = lat_ref[row * TM + b].astype(F32)
            moved = pltpu.roll(x, late, 0)
            x = jnp.where(sub < late, jnp.broadcast_to(x[0:1], (8, 128)), moved)
            blocks.append([pltpu.roll(x, (128 - 16 * (m - 1)) % 128, 1) for m in range(8)])
        turned.append(blocks)

    def piece(q, c, up):
        b, m = c // 8, c % 8
        k = (m + 4) % 8 if up else m
        base = 64 if up else 0
        own = turned[q][b][k]
        if m == 0:
            other = turned[q][b - 1][k] if b else turned[q][0][(k + 1) % 8]
            own = jnp.where(lane < base + 16, other, own)
        if m == 7:
            other = turned[q][b + 1][k] if b < 3 else turned[q][3][(k + 7) % 8]
            own = jnp.where(lane >= base + 32, other, own)
        return own

    for q in range(5):
        for c in range(W):
            low = piece(q, c, False)
            if q < 4:
                high = jnp.where((lane >= 64) & (lane < 112), piece(q + 1, c, True), 0.0)
            else:
                high = jnp.zeros((8, 128), F32)
            pat_ref[q, pl.ds(c, 8, stride=W), :] = jnp.where(lane < 48, low, high)


def merged(taps):
    wide = {place: value.astype(F32) for place, value in taps.items()}
    total = [wide[j, 0] + wide[j, 1] + wide[j, 2] for j in range(3)]
    values = {
        (0, 0, 1): total[0],
        (0, 1, 0): wide[1, 0] + wide[2, 0],
        (0, 1, 1): total[1] + total[2],
        (0, 1, 2): wide[1, 2] + wide[2, 2],
        (1, 0, 0): wide[0, 0] + wide[1, 0],
        (1, 0, 1): total[0] + total[1],
        (1, 0, 2): wide[0, 2] + wide[1, 2],
        (1, 1, 1): total[2],
    }
    values.update({p: wide[tap] for p, tap in RAW.items()})
    return values


def add_taps(raw, summed, i, rows):
    taps = {(j, k): raw[i, j, k, rows, :] for j in range(3) for k in range(3)}
    values = merged(taps)
    for n, p in enumerate(SUMS):
        summed[i, n, rows, :] = values[p].astype(BF16)


def tap_matrix(raw, summed, rp, b):
    parts = []
    for u in range(2):
        for i in range(3):
            if (rp, u, b) in RAW:
                j, k = RAW[rp, u, b]
                parts.append(raw[i, j, k])
            else:
                parts.append(summed[i, SUMS.index((rp, u, b))])
    return jnp.concatenate(parts, axis=0)


def add_timed_taps(raw, summed, rows, lanes):
    steps = [
        merged({(j, k): raw[i, j, k, rows, lanes] for j in range(3) for k in range(3)})
        for i in range(3)
    ]
    for p in PLACES:
        g0, g1, g2 = (step[p] for step in steps)
        outer, inner = 0.5 * (g0 + g2), 0.5 * g1
        for n, value in enumerate((g0, outer + inner, outer - inner, g2)):
            if (n, p) in KEPT:
                summed[KEPT.index((n, p)), rows, lanes] = value.astype(BF16)


def timed_matrix(raw, summed, rp, b, n):
    parts = []
    for u in range(2):
        p = (rp, u, b)
        if (n, p) in KEPT:
            parts.append(summed[KEPT.index((n, p))])
        else:
            j, k = RAW[p]
            parts.append(raw[0 if n == 0 else 2, j, k])
    return jnp.concatenate(parts, axis=0)


def gather_kernel(
    x_hbm, w1_hbm, w2_hbm, w3_hbm,
    lat, w1, w2, w2s, w3, w3s,
    send_sem, recv_sem, own_sem, sem1, sem2, sem3,
):
    s, t = lax.axis_index("seq"), lax.axis_index("tm")

    def away(d, e):
        return (s + d, lax.rem(t + e, TM))

    def when_row(d):
        if d == 0:
            return lambda f: f()
        return pl.when(s + d >= 0 if d < 0 else s + d < SEQ)

    barrier = pltpu.get_barrier_semaphore()
    for d, e in PEERS:

        @when_row(d)
        def _():
            pl.semaphore_signal(barrier, inc=1, device_id=away(d, e), device_id_type=MESH)

    own = lat.at[2 * TM + t]
    own_copy = pltpu.make_async_copy(x_hbm, own, own_sem)
    own_copy.start()

    parts = [pl.ds(128 * i, 128) for i in range(C1 // 128)]
    copies2 = [
        pltpu.make_async_copy(
            w2_hbm.at[:, :, :, part, :], w2.at[:, :, :, part, :], sem2.at[i]
        )
        for i, part in enumerate(parts)
    ]
    copy1 = pltpu.make_async_copy(
        w1_hbm, w1.at[:, pl.ds(0, 3), pl.ds(0, 48), :], sem1
    )
    copy3 = pltpu.make_async_copy(w3_hbm, w3, sem3)
    for copy in copies2:
        copy.start(priority=1)
    for i in range(3):
        w1[i, 3] = jnp.zeros((64, C1), BF16)
        for j in range(3):
            w1[i, j, 48:64, :] = jnp.zeros((16, C1), BF16)
    copy1.start(priority=1)
    copy3.start(priority=1)

    rows = 1 + jnp.minimum(s, 2) + jnp.minimum(SEQ - 1 - s, 2)
    own_copy.wait()
    pl.semaphore_wait(barrier, TM * rows - 1)
    for d, e in PEERS:

        @when_row(d)
        def _():
            pltpu.make_async_remote_copy(
                src_ref=own,
                dst_ref=lat.at[(2 - d) * TM + t],
                send_sem=send_sem.at[2 + d],
                recv_sem=recv_sem.at[2 - d],
                device_id=away(d, e),
                device_id_type=MESH,
            ).start()

    def all_of(d):
        some = lat.at[pl.ds(0, TM if d else TM - 1)]
        return pltpu.make_async_remote_copy(
            src_ref=some,
            dst_ref=some,
            send_sem=send_sem.at[2 + d],
            recv_sem=recv_sem.at[2 + d],
            device_id=away(0, 1),
            device_id_type=MESH,
        )

    for i, copy in enumerate(copies2):
        copy.wait()

        @pl.loop(0, 128 // CHUNK)
        def _(n):
            rows = pl.ds(pl.multiple_of(128 * i + CHUNK * n, CHUNK), CHUNK)
            for lane in range(0, C2, 128):
                add_timed_taps(w2, w2s, rows, pl.ds(lane, 128))

    copy3.wait()

    @pl.loop(0, C2 // 32)
    def _(n):
        for i in range(3):
            add_taps(w3, w3s, i, pl.ds(pl.multiple_of(32 * n, 32), 32))

    copy1.wait()
    for d in (0, 1, -1, 2, -2):

        @when_row(d)
        def _():
            all_of(d).wait_recv()

    for d in (0, 1, -1, 2, -2):

        @when_row(d)
        def _():
            all_of(d).wait_send()


def convolutions(s, pat, w1, w2, w2s, b1_ref, g1_ref, b2_ref, g2_ref, x1, x2, first):
    start = 4 if first else 0
    size = W * (6 - start)
    for r in range(3):
        q = jnp.clip(s - 1 + r, 0, SEQ - 1) - s + 1
        cols = []
        for i in range(3):
            for two in (0, 2):
                at = W * (i + start)
                cols.append(pat[q + two, at : at + size, :].astype(BF16))
        lhs = jnp.concatenate(cols, axis=1)
        hidden = jnp.dot(lhs, w1[...].reshape(768, C1), preferred_element_type=F32)
        act = silu_normed(hidden + b1_ref[...], g1_ref[...])
        kinds = (1, 3) if first else (0, 1, 2, 3)
        d = {k: act[W * (k - start) : W * (k - start) + W] for k in range(start, 6)}
        for k in range(first, start):
            d[k] = d[start]
        for f in range(first, 4, 2):
            terms = (d[f] - d[f + 2], d[f + 1] + d[f + 2], d[f + 2] - d[f + 1], d[f + 1] - d[f + 3])
            for n in kinds:
                x1[n, r, W // 2 * f : W // 2 * f + W, :] = terms[n]

    size = W * (4 - first) // 2
    lhs = {
        n: jnp.concatenate(
            [
                x1[n, u : u + 2, W // 2 * first : 2 * W, :].reshape(2 * size, C1)
                for u in range(2)
            ],
            axis=1,
        )
        for n in kinds
    }
    col = lax.broadcasted_iota(jnp.int32, (2 * size, 1), 0) % W

    def two_frames(rp, b):
        m = {
            n: jnp.dot(lhs[n], timed_matrix(w2, w2s, rp, b, n), preferred_element_type=F32)
            for n in kinds
        }
        if first:
            return m[1], m[1] - m[3]
        return m[0] + (m[1] + m[2]), (m[1] - m[2]) - m[3]

    for rp in range(2):
        for later, (q0, qk, q2) in enumerate(zip(*[two_frames(rp, b) for b in range(3)])):
            qk = qk + b2_ref[...]
            even = qk + jnp.where(col == 0, 0.0, pltpu.roll(q0, 1, 0) - q0)
            odd = qk + jnp.where(col == W - 1, 0.0, pltpu.roll(q2, 2 * size - 1, 0) - q2)
            for p, value in enumerate((even, odd)):
                act = silu_normed(value, g2_ref[...])
                for row in range(2):
                    slot = 2 * row + 1 - rp
                    for f in range(first, 4, 2):
                        part = act[size * row + W // 2 * (f - first) :][:W]
                        at = 64 * (f + later) + W * p
                        x2[slot, at : at + W, :] = part


def decode_kernel(
    lat, w1, w2, w2s, w3, w3s, b1_ref, g1_ref, b2_ref, g2_ref, b3_ref,
    out_ref,
    pat, x1, x2, o32,
):
    s, t = lax.axis_index("seq"), lax.axis_index("tm")

    patches(lat, pat, s, t)

    @pl.when(t == 0)
    def _():
        convolutions(s, pat, w1, w2, w2s, b1_ref, g1_ref, b2_ref, g2_ref, x1, x2, 2)
        for slot in range(4):
            third = x2[slot, 128:192, :]
            x2[slot, 0:64, :] = third
            x2[slot, 64:128, :] = third

    @pl.when(t > 0)
    def _():
        convolutions(s, pat, w1, w2, w2s, b1_ref, g1_ref, b2_ref, g2_ref, x1, x2, 0)

    slots = [jnp.where(s == 0, 1, 0), 1, 2, jnp.where(s == SEQ - 1, 2, 3)]
    col = lax.broadcasted_iota(jnp.int32, (32, 1), 0)
    for rp in range(2):
        lhs = jnp.concatenate(
            [
                jnp.concatenate(
                    [x2[slots[rp + u + row], 64 * i : 64 * i + 128, :] for row in range(2)],
                    axis=0,
                )
                for u in range(2)
                for i in range(3)
            ],
            axis=1,
        )
        rhs = jnp.concatenate([tap_matrix(w3, w3s, rp, b) for b in range(3)], axis=1)
        res = jnp.dot(lhs, rhs, preferred_element_type=F32)
        for row in range(2):
            for f in range(2):
                base = 128 * row + 64 * f
                (e0, ek, e2), (o0, ok, o2) = [
                    [
                        res[base + 32 * p : base + 32 * p + 32, C3 * b : C3 * b + C3]
                        for b in range(3)
                    ]
                    for p in range(2)
                ]
                ek = ek + b3_ref[...]
                ok = ok + b3_ref[...]
                values = (
                    ek + jnp.where(col == 0, 0.0, pltpu.roll(o0, 1, 0) - e0),
                    ek + (o2 - e2),
                    ok + (e0 - o0),
                    ok + jnp.where(col == W - 1, 0.0, pltpu.roll(e2, 31, 0) - o2),
                )
                for n, value in enumerate(values):
                    o32[f, 2 * row + rp, pl.ds(n, W, stride=4), :] = value
    out_ref[...] = o32[...].astype(BF16)


def per_device(latent, w1, b1, g1, w2, b2, g2, w3, b3):
    line = lambda v: v.reshape(1, -1)
    vmem = pl.BlockSpec(memory_space=pltpu.VMEM)
    hbm = pl.BlockSpec(memory_space=pltpu.HBM)
    in_hbm = lambda v: pltpu.with_memory_space_constraint(v, pltpu.HBM)
    kept = pl.pallas_call(
        gather_kernel,
        out_shape=[
            pltpu.VMEM((5 * TM, 8, 128), BF16),
            pltpu.VMEM((3, 4, 64, C1), BF16),
            pltpu.VMEM((3, 3, 3, C1, C2), BF16),
            pltpu.VMEM((len(KEPT), C1, C2), BF16),
            pltpu.VMEM((3, 3, 3, C2, C3), BF16),
            pltpu.VMEM((3, 8, C2, C3), BF16),
        ],
        in_specs=[hbm] * 4,
        out_specs=[vmem] * 6,
        scratch_shapes=[
            pltpu.SemaphoreType.DMA((5,)),
            pltpu.SemaphoreType.DMA((5,)),
            pltpu.SemaphoreType.DMA,
            pltpu.SemaphoreType.DMA,
            pltpu.SemaphoreType.DMA((C1 // 128,)),
            pltpu.SemaphoreType.DMA,
        ],
        compiler_params=pltpu.CompilerParams(
            collective_id=0, has_side_effects=True, vmem_limit_bytes=8 << 20
        ),
        name="gather",
    )(*map(in_hbm, (latent, w1.reshape(3, 3, 48, C1), w2, w3)))
    return pl.pallas_call(
        decode_kernel,
        out_shape=jax.ShapeDtypeStruct((2, 4, 128, C3), BF16),
        in_specs=[vmem] * 11,
        out_specs=vmem,
        scratch_shapes=[
            pltpu.VMEM((5, 8 * W, 128), F32),
            pltpu.VMEM((4, 3, 2 * W, C1), BF16),
            pltpu.VMEM((4, 4 * 64, C2), BF16),
            pltpu.VMEM((2, 4, 128, C3), F32),
        ],
        compiler_params=pltpu.CompilerParams(vmem_limit_bytes=24 << 20),
        name="decode",
    )(*kept, line(b1), line(g1), line(b2), line(g2), line(b3))


def solution(mesh):
    placed = (P(None, ("seq", "tm")), P(), P(), P(), P(), P(), P(), P(), P())
    return jax.shard_map(
        per_device,
        mesh=mesh,
        in_specs=placed,
        out_specs=P("tm", "seq", None, None),
        check_vma=False,
    )
```

```python
import jax
import jax.numpy as jnp
from jax import lax
from jax.experimental import pallas as pl
from jax.experimental.pallas import tpu as pltpu
from jax.sharding import PartitionSpec as P

MESH = pl.DeviceIdType.MESH
F32 = jnp.float32
BF16 = jnp.bfloat16

SEQ = 32
TM = 4
W = 32
CHUNK = 32
C1, C2, C3 = 512, 256, 128
EPS = 1e-06

RAW = {(0, 0, 0): (0, 0), (0, 0, 2): (0, 2), (1, 1, 0): (2, 0), (1, 1, 2): (2, 2)}
SUMS = ((0, 0, 1), (0, 1, 0), (0, 1, 1), (0, 1, 2), (1, 0, 0), (1, 0, 1), (1, 0, 2), (1, 1, 1))
PLACES = SUMS + tuple(RAW)
KEPT = tuple((n, p) for n in range(4) for p in (SUMS if n in (0, 3) else PLACES))
PEERS = tuple(
    (d, e) for d, e in (
        (2, 2), (-2, 2), (1, 2), (-1, 2), (2, 1), (2, 3), (-2, 1), (-2, 3), (0, 2), (1, 1), (1, 3),
        (-1, 1), (-1, 3), (2, 0), (-2, 0), (0, 1), (0, 3), (1, 0), (-1, 0),
    )
)


def silu_normed(hidden, gain):
    factor = lax.rsqrt(jnp.mean(hidden * hidden, axis=1, keepdims=True) + EPS)
    half = hidden * factor * (0.5 * gain)
    return (half + half * jnp.tanh(half)).astype(BF16)


def patches(lat_ref, pat_ref, s, t):
    late = 6 - 2 * t
    sub = lax.broadcasted_iota(jnp.int32, (8, 128), 0)
    lane = lax.broadcasted_iota(jnp.int32, (8, 128), 1)
    turned = []
    for q in range(5):
        row = jnp.clip(s - 2 + q, 0, SEQ - 1) - s + 2
        blocks = []
        for b in range(TM):
            x = lat_ref[row * TM + b].astype(F32)
            moved = pltpu.roll(x, late, 0)
            x = jnp.where(sub < late, jnp.broadcast_to(x[0:1], (8, 128)), moved)
            blocks.append([pltpu.roll(x, (128 - 16 * (m - 1)) % 128, 1) for m in range(8)])
        turned.append(blocks)

    def piece(q, c, up):
        b, m = c // 8, c % 8
        k = (m + 4) % 8 if up else m
        base = 64 if up else 0
        own = turned[q][b][k]
        if m == 0:
            other = turned[q][b - 1][k] if b else turned[q][0][(k + 1) % 8]
            own = jnp.where(lane < base + 16, other, own)
        if m == 7:
            other = turned[q][b + 1][k] if b < 3 else turned[q][3][(k + 7) % 8]
            own = jnp.where(lane >= base + 32, other, own)
        return own

    for q in range(5):
        for c in range(W):
            low = piece(q, c, False)
            if q < 4:
                high = jnp.where((lane >= 64) & (lane < 112), piece(q + 1, c, True), 0.0)
            else:
                high = jnp.zeros((8, 128), F32)
            pat_ref[q, pl.ds(c, 8, stride=W), :] = jnp.where(lane < 48, low, high)


def merged(taps):
    wide = {place: value.astype(F32) for place, value in taps.items()}
    total = [wide[j, 0] + wide[j, 1] + wide[j, 2] for j in range(3)]
    values = {
        (0, 0, 1): total[0],
        (0, 1, 0): wide[1, 0] + wide[2, 0],
        (0, 1, 1): total[1] + total[2],
        (0, 1, 2): wide[1, 2] + wide[2, 2],
        (1, 0, 0): wide[0, 0] + wide[1, 0],
        (1, 0, 1): total[0] + total[1],
        (1, 0, 2): wide[0, 2] + wide[1, 2],
        (1, 1, 1): total[2],
    }
    values.update({p: wide[tap] for p, tap in RAW.items()})
    return values


def add_timed_taps(raw, summed, rows, lanes):
    steps = [
        merged({(j, k): raw[i, j, k, rows, lanes] for j in range(3) for k in range(3)})
        for i in range(3)
    ]
    for p in PLACES:
        g0, g1, g2 = (step[p] for step in steps)
        outer = g0 + g2
        for n, value in enumerate((g0, outer + g1, outer - g1, g2)):
            if (n, p) in KEPT:
                summed[KEPT.index((n, p)), rows, lanes] = value.astype(BF16)


def timed_matrix(raw, summed, rp, b, n):
    parts = []
    for u in range(2):
        p = (rp, u, b)
        if (n, p) in KEPT:
            parts.append(summed[KEPT.index((n, p))])
        else:
            j, k = RAW[p]
            parts.append(raw[0 if n == 0 else 2, j, k])
    return jnp.concatenate(parts, axis=0)


def gather_kernel(
    x_hbm, w1_hbm, w2_hbm, w3_hbm,
    lat, w1, w2, w2s, w3, w3s,
    send_sem, recv_sem, own_sem, sem1, sem2, sem3,
):
    s, t = lax.axis_index("seq"), lax.axis_index("tm")

    def away(d, e):
        return (s + d, lax.rem(t + e, TM))

    def when_row(d):
        if d == 0:
            return lambda f: f()
        return pl.when(s + d >= 0 if d < 0 else s + d < SEQ)

    barrier = pltpu.get_barrier_semaphore()
    for d, e in PEERS:

        @when_row(d)
        def _():
            pl.semaphore_signal(barrier, inc=1, device_id=away(d, e), device_id_type=MESH)

    own = lat.at[2 * TM + t]
    own_copy = pltpu.make_async_copy(x_hbm, own, own_sem)
    own_copy.start()

    parts = [pl.ds(128 * i, 128) for i in range(C1 // 128)]
    copies2 = [
        pltpu.make_async_copy(
            w2_hbm.at[:, :, :, part, :], w2.at[:, :, :, part, :], sem2.at[i]
        )
        for i, part in enumerate(parts)
    ]
    copy1 = pltpu.make_async_copy(
        w1_hbm, w1.at[:, pl.ds(0, 3), pl.ds(0, 48), :], sem1
    )
    copy3 = pltpu.make_async_copy(w3_hbm, w3, sem3)
    for copy in copies2:
        copy.start(priority=1)
    for i in range(3):
        w1[i, 3] = jnp.zeros((64, C1), BF16)
        for j in range(3):
            w1[i, j, 48:64, :] = jnp.zeros((16, C1), BF16)
    copy1.start(priority=1)
    copy3.start(priority=1)

    rows = 1 + jnp.minimum(s, 2) + jnp.minimum(SEQ - 1 - s, 2)
    own_copy.wait()
    pl.semaphore_wait(barrier, TM * rows - 1)
    for d, e in PEERS:

        @when_row(d)
        def _():
            pltpu.make_async_remote_copy(
                src_ref=own,
                dst_ref=lat.at[(2 - d) * TM + t],
                send_sem=send_sem.at[2 + d],
                recv_sem=recv_sem.at[2 - d],
                device_id=away(d, e),
                device_id_type=MESH,
            ).start()

    def all_of(d):
        some = lat.at[pl.ds(0, TM if d else TM - 1)]
        return pltpu.make_async_remote_copy(
            src_ref=some,
            dst_ref=some,
            send_sem=send_sem.at[2 + d],
            recv_sem=recv_sem.at[2 + d],
            device_id=away(0, 1),
            device_id_type=MESH,
        )

    for i, copy in enumerate(copies2):
        copy.wait()

        @pl.loop(0, 128 // CHUNK)
        def _(n):
            rows = pl.ds(pl.multiple_of(128 * i + CHUNK * n, CHUNK), CHUNK)
            for lane in range(0, C2, 128):
                add_timed_taps(w2, w2s, rows, pl.ds(lane, 128))

    copy3.wait()

    @pl.loop(0, C2 // CHUNK)
    def _(n):
        add_timed_taps(w3, w3s, pl.ds(pl.multiple_of(CHUNK * n, CHUNK), CHUNK), pl.ds(0, C3))

    copy1.wait()
    for d in (0, 1, -1, 2, -2):

        @when_row(d)
        def _():
            all_of(d).wait_recv()

    for d in (0, 1, -1, 2, -2):

        @when_row(d)
        def _():
            all_of(d).wait_send()


def timed_terms(d):
    half1, half2 = d[1] * 0.5, d[2] * 0.5
    return d[0] - d[2], half1 + half2, half2 - half1, d[1] - d[3]


def convolutions(
    s, pat, w1, w2, w2s, w3, w3s, b1_ref, g1_ref, b2_ref, g2_ref, b3_ref, x1, x2, o32, first
):
    start = 4 if first else 0
    size = W * (6 - start)
    def first_hidden(r):
        q = jnp.clip(s - 1 + r, 0, SEQ - 1) - s + 1
        cols = []
        for i in range(3):
            for two in (0, 2):
                at = W * (i + start)
                cols.append(pat[q + two, at : at + size, :].astype(BF16))
        lhs = jnp.concatenate(cols, axis=1)
        return jnp.dot(lhs, w1[...].reshape(768, C1), preferred_element_type=F32)

    hidden = [first_hidden(r) for r in range(3)]
    for r in range(3):
        act = silu_normed(hidden[r] + b1_ref[...], g1_ref[...])
        kinds = (1, 3) if first else (0, 1, 2, 3)
        d = {k: act[W * (k - start) : W * (k - start) + W] for k in range(start, 6)}
        for k in range(first, start):
            d[k] = d[start]
        for f in range(first, 4, 2):
            terms = timed_terms([d[f + k] for k in range(4)])
            for n in kinds:
                x1[n, r, W // 2 * f : W // 2 * f + W, :] = terms[n]

    size = W * (4 - first) // 2
    lhs = {
        n: jnp.concatenate(
            [
                x1[n, u : u + 2, W // 2 * first : 2 * W, :].reshape(2 * size, C1)
                for u in range(2)
            ],
            axis=1,
        )
        for n in kinds
    }
    col = lax.broadcasted_iota(jnp.int32, (2 * size, 1), 0) % W

    def two_frames(rp, b):
        m = {
            n: jnp.dot(lhs[n], timed_matrix(w2, w2s, rp, b, n), preferred_element_type=F32)
            for n in kinds
        }
        if first:
            return m[1], m[1] - m[3]
        return m[0] + (m[1] + m[2]), (m[1] - m[2]) - m[3]

    acts = {}
    for rp in range(2):
        for later, (q0, qk, q2) in enumerate(zip(*[two_frames(rp, b) for b in range(3)])):
            qk = qk + b2_ref[...]
            even = qk + jnp.where(col == 0, 0.0, pltpu.roll(q0, 1, 0) - q0)
            odd = qk + jnp.where(col == W - 1, 0.0, pltpu.roll(q2, 2 * size - 1, 0) - q2)
            for p, value in enumerate((even, odd)):
                act = silu_normed(value, g2_ref[...])
                for row in range(2):
                    for f in range(first, 4, 2):
                        part = act[size * row + W // 2 * (f - first) :][:W]
                        acts[2 * row + 1 - rp, p, f + later] = part
        for slot, p in [(2 * row + 1 - rp, p) for row in range(2) for p in range(2)]:
            d = [acts[slot, p, f if f >= first else first] for f in range(4)]
            terms = timed_terms(d)
            for n in kinds:
                x2[n, slot, W * p : W * p + W, :] = terms[n]

    slots = [jnp.where(s == 0, 1, 0), 1, 2, jnp.where(s == SEQ - 1, 2, 3)]
    col = lax.broadcasted_iota(jnp.int32, (32, 1), 0)
    for rp in range(2):
        m = {}
        for n in kinds:
            lhs = jnp.concatenate(
                [
                    jnp.concatenate([x2[n, slots[rp + u + row]] for row in range(2)], axis=0)
                    for u in range(2)
                ],
                axis=1,
            )
            taps = jnp.concatenate([timed_matrix(w3, w3s, rp, b, n) for b in range(3)], axis=1)
            m[n] = jnp.dot(lhs, taps, preferred_element_type=F32)
        if first:
            frames = m[1], m[1] - m[3]
        else:
            frames = m[0] + (m[1] + m[2]), (m[1] - m[2]) - m[3]
        for f, res in enumerate(frames):
            for row in range(2):
                base = 64 * row
                (e0, ek, e2), (o0, ok, o2) = [
                    [
                        res[base + 32 * p : base + 32 * p + 32, C3 * b : C3 * b + C3]
                        for b in range(3)
                    ]
                    for p in range(2)
                ]
                ek = ek + b3_ref[...]
                ok = ok + b3_ref[...]
                values = (
                    ek + jnp.where(col == 0, 0.0, pltpu.roll(o0, 1, 0) - e0),
                    ek + (o2 - e2),
                    ok + (e0 - o0),
                    ok + jnp.where(col == W - 1, 0.0, pltpu.roll(e2, 31, 0) - o2),
                )
                for n, value in enumerate(values):
                    o32[f, 2 * row + rp, pl.ds(n, W, stride=4), :] = value

def decode_kernel(
    lat, w1, w2, w2s, w3, w3s, b1_ref, g1_ref, b2_ref, g2_ref, b3_ref,
    out_ref,
    pat, x1, x2, o32,
):
    s, t = lax.axis_index("seq"), lax.axis_index("tm")

    patches(lat, pat, s, t)
    refs = (pat, w1, w2, w2s, w3, w3s, b1_ref, g1_ref, b2_ref, g2_ref, b3_ref, x1, x2, o32)

    @pl.when(t == 0)
    def _():
        convolutions(s, *refs, 2)

    @pl.when(t > 0)
    def _():
        convolutions(s, *refs, 0)

    out_ref[...] = o32[...].astype(BF16)


def per_device(latent, w1, b1, g1, w2, b2, g2, w3, b3):
    line = lambda v: v.reshape(1, -1)
    vmem = pl.BlockSpec(memory_space=pltpu.VMEM)
    hbm = pl.BlockSpec(memory_space=pltpu.HBM)
    in_hbm = lambda v: pltpu.with_memory_space_constraint(v, pltpu.HBM)
    kept = pl.pallas_call(
        gather_kernel,
        out_shape=[
            pltpu.VMEM((5 * TM, 8, 128), BF16),
            pltpu.VMEM((3, 4, 64, C1), BF16),
            pltpu.VMEM((3, 3, 3, C1, C2), BF16),
            pltpu.VMEM((len(KEPT), C1, C2), BF16),
            pltpu.VMEM((3, 3, 3, C2, C3), BF16),
            pltpu.VMEM((len(KEPT), C2, C3), BF16),
        ],
        in_specs=[hbm] * 4,
        out_specs=[vmem] * 6,
        scratch_shapes=[
            pltpu.SemaphoreType.DMA((5,)),
            pltpu.SemaphoreType.DMA((5,)),
            pltpu.SemaphoreType.DMA,
            pltpu.SemaphoreType.DMA,
            pltpu.SemaphoreType.DMA((C1 // 128,)),
            pltpu.SemaphoreType.DMA,
        ],
        compiler_params=pltpu.CompilerParams(
            collective_id=0, has_side_effects=True, vmem_limit_bytes=8 << 20
        ),
        name="gather",
    )(*map(in_hbm, (latent, w1.reshape(3, 3, 48, C1), w2, w3)))
    return pl.pallas_call(
        decode_kernel,
        out_shape=jax.ShapeDtypeStruct((2, 4, 128, C3), BF16),
        in_specs=[vmem] * 11,
        out_specs=vmem,
        scratch_shapes=[
            pltpu.VMEM((5, 8 * W, 128), F32),
            pltpu.VMEM((4, 3, 2 * W, C1), BF16),
            pltpu.VMEM((4, 4, 2 * W, C2), BF16),
            pltpu.VMEM((2, 4, 128, C3), F32),
        ],
        compiler_params=pltpu.CompilerParams(vmem_limit_bytes=24 << 20),
        name="decode",
    )(*kept, line(b1), line(g1), line(b2), line(g2), line(b3))


def solution(mesh):
    placed = (P(None, ("seq", "tm")), P(), P(), P(), P(), P(), P(), P(), P())
    return jax.shard_map(
        per_device,
        mesh=mesh,
        in_specs=placed,
        out_specs=P("tm", "seq", None, None),
        check_vma=False,
    )
```

```python
import jax
import jax.numpy as jnp
from jax import lax
from jax.experimental import pallas as pl
from jax.experimental.pallas import tpu as pltpu
from jax.sharding import PartitionSpec as P

MESH = pl.DeviceIdType.MESH
F32 = jnp.float32
BF16 = jnp.bfloat16

SEQ = 32
TM = 4
W = 32
CHUNK = 32
C1, C2, C3 = 512, 256, 128
EPS = 1e-06

RAW = {(0, 0, 0): (0, 0), (0, 0, 2): (0, 2), (1, 1, 0): (2, 0), (1, 1, 2): (2, 2)}
SUMS = ((0, 0, 1), (0, 1, 0), (0, 1, 1), (0, 1, 2), (1, 0, 0), (1, 0, 1), (1, 0, 2), (1, 1, 1))
PLACES = SUMS + tuple(RAW)
KEPT = tuple((n, p) for n in range(4) for p in (SUMS if n in (0, 3) else PLACES))
PEERS = tuple(
    (d, e) for d, e in (
        (2, 2), (-2, 2), (1, 2), (-1, 2), (2, 1), (2, 3), (-2, 1), (-2, 3), (0, 2), (1, 1), (1, 3),
        (-1, 1), (-1, 3), (2, 0), (-2, 0), (0, 1), (0, 3), (1, 0), (-1, 0),
    )
)


def silu_normed(hidden, gain):
    factor = lax.rsqrt(jnp.mean(hidden * hidden, axis=1, keepdims=True) + EPS)
    half = hidden * factor * (0.5 * gain)
    return (half + half * jnp.tanh(half)).astype(BF16)


def patches(lat_ref, pat_ref, s, t):
    late = 6 - 2 * t
    sub = lax.broadcasted_iota(jnp.int32, (8, 128), 0)
    lane = lax.broadcasted_iota(jnp.int32, (8, 128), 1)
    turned = []
    for q in range(5):
        row = jnp.clip(s - 2 + q, 0, SEQ - 1) - s + 2
        blocks = []
        for b in range(TM):
            x = lat_ref[row * TM + b].astype(F32)
            moved = pltpu.roll(x, late, 0)
            x = jnp.where(sub < late, jnp.broadcast_to(x[0:1], (8, 128)), moved)
            blocks.append([pltpu.roll(x, (128 - 16 * (m - 1)) % 128, 1) for m in range(8)])
        turned.append(blocks)

    def piece(q, c, up):
        b, m = c // 8, c % 8
        k = (m + 4) % 8 if up else m
        base = 64 if up else 0
        own = turned[q][b][k]
        if m == 0:
            other = turned[q][b - 1][k] if b else turned[q][0][(k + 1) % 8]
            own = jnp.where(lane < base + 16, other, own)
        if m == 7:
            other = turned[q][b + 1][k] if b < 3 else turned[q][3][(k + 7) % 8]
            own = jnp.where(lane >= base + 32, other, own)
        return own

    for q in range(5):
        for c in range(W):
            low = piece(q, c, False)
            if q < 4:
                high = jnp.where((lane >= 64) & (lane < 112), piece(q + 1, c, True), 0.0)
            else:
                high = jnp.zeros((8, 128), F32)
            pat_ref[q, pl.ds(c, 8, stride=W), :] = jnp.where(lane < 48, low, high)


def merged(taps):
    wide = {place: value.astype(F32) for place, value in taps.items()}
    total = [wide[j, 0] + wide[j, 1] + wide[j, 2] for j in range(3)]
    values = {
        (0, 0, 1): total[0],
        (0, 1, 0): wide[1, 0] + wide[2, 0],
        (0, 1, 1): total[1] + total[2],
        (0, 1, 2): wide[1, 2] + wide[2, 2],
        (1, 0, 0): wide[0, 0] + wide[1, 0],
        (1, 0, 1): total[0] + total[1],
        (1, 0, 2): wide[0, 2] + wide[1, 2],
        (1, 1, 1): total[2],
    }
    values.update({p: wide[tap] for p, tap in RAW.items()})
    return values


def add_timed_taps(raw, summed, rows, half):
    lanes = pl.ds(128 * half, 128)
    steps = [
        merged({(j, k): raw[i, j, k, rows, lanes] for j in range(3) for k in range(3)})
        for i in range(3)
    ]
    for p in PLACES:
        g0, g1, g2 = (step[p] for step in steps)
        outer = g0 + g2
        for n, value in enumerate((g0, outer + g1, outer - g1, g2)):
            if (n, p) in KEPT:
                summed[KEPT.index((n, p)), half, rows, :] = value.astype(BF16)


def timed_matrix(raw, summed, rp, b, n):
    parts = []
    for u in range(2):
        p = (rp, u, b)
        if (n, p) in KEPT:
            kept = KEPT.index((n, p))
            halves = [summed[kept, half] for half in range(summed.shape[1])]
            parts.append(jnp.concatenate(halves, axis=1))
        else:
            j, k = RAW[p]
            parts.append(raw[0 if n == 0 else 2, j, k])
    return jnp.concatenate(parts, axis=0)


def gather_kernel(
    x_hbm, w1_hbm, w2_hbm, w3_hbm,
    lat, w1, w2, w2s, w3, w3s,
    send_sem, recv_sem, own_sem, sem1, sem2, sem3,
):
    s, t = lax.axis_index("seq"), lax.axis_index("tm")

    def away(d, e):
        return (s + d, lax.rem(t + e, TM))

    def when_row(d):
        if d == 0:
            return lambda f: f()
        return pl.when(s + d >= 0 if d < 0 else s + d < SEQ)

    barrier = pltpu.get_barrier_semaphore()
    for d, e in PEERS:

        @when_row(d)
        def _():
            pl.semaphore_signal(barrier, inc=1, device_id=away(d, e), device_id_type=MESH)

    own = lat.at[2 * TM + t]
    own_copy = pltpu.make_async_copy(x_hbm, own, own_sem)
    own_copy.start()

    parts = [pl.ds(128 * i, 128) for i in range(C1 // 128)]
    copies2 = [
        pltpu.make_async_copy(
            w2_hbm.at[:, :, :, part, :], w2.at[:, :, :, part, :], sem2.at[i]
        )
        for i, part in enumerate(parts)
    ]
    copy1 = pltpu.make_async_copy(
        w1_hbm, w1.at[:, pl.ds(0, 3), pl.ds(0, 48), :], sem1
    )
    copy3 = pltpu.make_async_copy(w3_hbm, w3, sem3)
    for copy in copies2:
        copy.start(priority=1)
    for i in range(3):
        w1[i, 3] = jnp.zeros((64, C1), BF16)
        for j in range(3):
            w1[i, j, 48:64, :] = jnp.zeros((16, C1), BF16)
    copy1.start(priority=1)
    copy3.start(priority=1)

    rows = 1 + jnp.minimum(s, 2) + jnp.minimum(SEQ - 1 - s, 2)
    own_copy.wait()
    pl.semaphore_wait(barrier, TM * rows - 1)
    for d, e in PEERS:

        @when_row(d)
        def _():
            pltpu.make_async_remote_copy(
                src_ref=own,
                dst_ref=lat.at[(2 - d) * TM + t],
                send_sem=send_sem.at[2 + d],
                recv_sem=recv_sem.at[2 - d],
                device_id=away(d, e),
                device_id_type=MESH,
            ).start()

    def all_of(d):
        some = lat.at[pl.ds(0, TM if d else TM - 1)]
        return pltpu.make_async_remote_copy(
            src_ref=some,
            dst_ref=some,
            send_sem=send_sem.at[2 + d],
            recv_sem=recv_sem.at[2 + d],
            device_id=away(0, 1),
            device_id_type=MESH,
        )

    for i, copy in enumerate(copies2):
        copy.wait()

        @pl.loop(0, 128 // CHUNK)
        def _(n):
            rows = pl.ds(pl.multiple_of(128 * i + CHUNK * n, CHUNK), CHUNK)
            for half in range(2):
                add_timed_taps(w2, w2s, rows, half)

    copy3.wait()

    @pl.loop(0, C2 // CHUNK)
    def _(n):
        add_timed_taps(w3, w3s, pl.ds(pl.multiple_of(CHUNK * n, CHUNK), CHUNK), 0)

    copy1.wait()
    for d in (0, 1, -1, 2, -2):

        @when_row(d)
        def _():
            all_of(d).wait_send()

    for d in (0, 1, -1, 2, -2):

        @when_row(d)
        def _():
            all_of(d).wait_recv()


def timed_terms(d):
    half1, half2 = d[1] * 0.5, d[2] * 0.5
    return d[0] - d[2], half1 + half2, half2 - half1, d[1] - d[3]


def convolutions(
    s, pat, w1, w2, w2s, w3, w3s, b1_ref, g1_ref, b2_ref, g2_ref, b3_ref, x1, x2, o32, first
):
    start = 4 if first else 0
    size = W * (6 - start)
    def first_hidden(r):
        q = jnp.clip(s - 1 + r, 0, SEQ - 1) - s + 1
        cols = []
        for i in range(3):
            for two in (0, 2):
                at = W * (i + start)
                cols.append(pat[q + two, at : at + size, :].astype(BF16))
        lhs = jnp.concatenate(cols, axis=1)
        return jnp.dot(lhs, w1[...].reshape(768, C1), preferred_element_type=F32)

    hidden = [first_hidden(r) for r in range(3)]
    for r in range(3):
        act = silu_normed(hidden[r] + b1_ref[...], g1_ref[...])
        kinds = (1, 3) if first else (0, 1, 2, 3)
        d = {k: act[W * (k - start) : W * (k - start) + W] for k in range(start, 6)}
        for k in range(first, start):
            d[k] = d[start]
        for f in range(first, 4, 2):
            terms = timed_terms([d[f + k] for k in range(4)])
            for n in kinds:
                x1[n, r, W // 2 * f : W // 2 * f + W, :] = terms[n]

    size = W * (4 - first) // 2
    lhs = {
        n: jnp.concatenate(
            [
                x1[n, u : u + 2, W // 2 * first : 2 * W, :].reshape(2 * size, C1)
                for u in range(2)
            ],
            axis=1,
        )
        for n in kinds
    }
    col = lax.broadcasted_iota(jnp.int32, (2 * size, 1), 0) % W

    def two_frames(rp, b):
        m = {
            n: jnp.dot(lhs[n], timed_matrix(w2, w2s, rp, b, n), preferred_element_type=F32)
            for n in kinds
        }
        if first:
            return m[1], m[1] - m[3]
        return m[0] + (m[1] + m[2]), (m[1] - m[2]) - m[3]

    acts = {}
    for rp in range(2):
        for later, (q0, qk, q2) in enumerate(zip(*[two_frames(rp, b) for b in range(3)])):
            qk = qk + b2_ref[...]
            even = qk + jnp.where(col == 0, 0.0, pltpu.roll(q0, 1, 0) - q0)
            odd = qk + jnp.where(col == W - 1, 0.0, pltpu.roll(q2, 2 * size - 1, 0) - q2)
            for p, value in enumerate((even, odd)):
                act = silu_normed(value, g2_ref[...])
                for row in range(2):
                    for f in range(first, 4, 2):
                        part = act[size * row + W // 2 * (f - first) :][:W]
                        acts[2 * row + 1 - rp, p, f + later] = part
        for slot, p in [(2 * row + 1 - rp, p) for row in range(2) for p in range(2)]:
            d = [acts[slot, p, f if f >= first else first] for f in range(4)]
            terms = timed_terms(d)
            for n in kinds:
                x2[n, slot, W * p : W * p + W, :] = terms[n]

    slots = [jnp.where(s == 0, 1, 0), 1, 2, jnp.where(s == SEQ - 1, 2, 3)]
    col = lax.broadcasted_iota(jnp.int32, (32, 1), 0)
    for rp in range(2):
        m = {}
        for n in kinds:
            lhs = jnp.concatenate(
                [
                    jnp.concatenate([x2[n, slots[rp + u + row]] for row in range(2)], axis=0)
                    for u in range(2)
                ],
                axis=1,
            )
            taps = jnp.concatenate([timed_matrix(w3, w3s, rp, b, n) for b in range(3)], axis=1)
            m[n] = jnp.dot(lhs, taps, preferred_element_type=F32)
        if first:
            frames = m[1], m[1] - m[3]
        else:
            frames = m[0] + (m[1] + m[2]), (m[1] - m[2]) - m[3]
        for f, res in enumerate(frames):
            for row in range(2):
                base = 64 * row
                (e0, ek, e2), (o0, ok, o2) = [
                    [
                        res[base + 32 * p : base + 32 * p + 32, C3 * b : C3 * b + C3]
                        for b in range(3)
                    ]
                    for p in range(2)
                ]
                ek = ek + b3_ref[...]
                ok = ok + b3_ref[...]
                values = (
                    ek + jnp.where(col == 0, 0.0, pltpu.roll(o0, 1, 0) - e0),
                    ek + (o2 - e2),
                    ok + (e0 - o0),
                    ok + jnp.where(col == W - 1, 0.0, pltpu.roll(e2, 31, 0) - o2),
                )
                for n, value in enumerate(values):
                    o32[f, 2 * row + rp, pl.ds(n, W, stride=4), :] = value

def decode_kernel(
    lat, w1, w2, w2s, w3, w3s, b1_ref, g1_ref, b2_ref, g2_ref, b3_ref,
    out_ref,
    pat, x1, x2, o32,
):
    s, t = lax.axis_index("seq"), lax.axis_index("tm")

    patches(lat, pat, s, t)
    refs = (pat, w1, w2, w2s, w3, w3s, b1_ref, g1_ref, b2_ref, g2_ref, b3_ref, x1, x2, o32)

    @pl.when(t == 0)
    def _():
        convolutions(s, *refs, 2)

    @pl.when(t > 0)
    def _():
        convolutions(s, *refs, 0)

    out_ref[...] = o32[...].astype(BF16)


def per_device(latent, w1, b1, g1, w2, b2, g2, w3, b3):
    line = lambda v: v.reshape(1, -1)
    vmem = pl.BlockSpec(memory_space=pltpu.VMEM)
    hbm = pl.BlockSpec(memory_space=pltpu.HBM)
    in_hbm = lambda v: pltpu.with_memory_space_constraint(v, pltpu.HBM)
    kept = pl.pallas_call(
        gather_kernel,
        out_shape=[
            pltpu.VMEM((5 * TM, 8, 128), BF16),
            pltpu.VMEM((3, 4, 64, C1), BF16),
            pltpu.VMEM((3, 3, 3, C1, C2), BF16),
            pltpu.VMEM((len(KEPT), 2, C1, 128), BF16),
            pltpu.VMEM((3, 3, 3, C2, C3), BF16),
            pltpu.VMEM((len(KEPT), 1, C2, C3), BF16),
        ],
        in_specs=[hbm] * 4,
        out_specs=[vmem] * 6,
        scratch_shapes=[
            pltpu.SemaphoreType.DMA((5,)),
            pltpu.SemaphoreType.DMA((5,)),
            pltpu.SemaphoreType.DMA,
            pltpu.SemaphoreType.DMA,
            pltpu.SemaphoreType.DMA((C1 // 128,)),
            pltpu.SemaphoreType.DMA,
        ],
        compiler_params=pltpu.CompilerParams(
            collective_id=0, has_side_effects=True, vmem_limit_bytes=8 << 20
        ),
        name="gather",
    )(*map(in_hbm, (latent, w1.reshape(3, 3, 48, C1), w2, w3)))
    return pl.pallas_call(
        decode_kernel,
        out_shape=jax.ShapeDtypeStruct((2, 4, 128, C3), BF16),
        in_specs=[vmem] * 11,
        out_specs=vmem,
        scratch_shapes=[
            pltpu.VMEM((5, 8 * W, 128), F32),
            pltpu.VMEM((4, 3, 2 * W, C1), BF16),
            pltpu.VMEM((4, 4, 2 * W, C2), BF16),
            pltpu.VMEM((2, 4, 128, C3), F32),
        ],
        compiler_params=pltpu.CompilerParams(vmem_limit_bytes=24 << 20),
        name="decode",
    )(*kept, line(b1), line(g1), line(b2), line(g2), line(b3))


def solution(mesh):
    placed = (P(None, ("seq", "tm")), P(), P(), P(), P(), P(), P(), P(), P())
    return jax.shard_map(
        per_device,
        mesh=mesh,
        in_specs=placed,
        out_specs=P("tm", "seq", None, None),
        check_vma=False,
    )
```

```python
import jax
import jax.numpy as jnp
from jax import lax
from jax.experimental import pallas as pl
from jax.experimental.pallas import tpu as pltpu
from jax.sharding import PartitionSpec as P

MESH = pl.DeviceIdType.MESH
F32 = jnp.float32
BF16 = jnp.bfloat16

SEQ = 32
TM = 4
W = 32
CHUNK = 32
C1, C2, C3 = 512, 256, 128
EPS = 1e-06

RAW = {(0, 0, 0): (0, 0), (0, 0, 2): (0, 2), (1, 1, 0): (2, 0), (1, 1, 2): (2, 2)}
SUMS = ((0, 0, 1), (0, 1, 0), (0, 1, 1), (0, 1, 2), (1, 0, 0), (1, 0, 1), (1, 0, 2), (1, 1, 1))
PLACES = SUMS + tuple(RAW)
KEPT = tuple((n, p) for n in range(4) for p in (SUMS if n in (0, 3) else PLACES))
PEERS = tuple(
    (d, e) for d, e in (
        (2, 2), (-2, 2), (1, 2), (-1, 2), (2, 1), (2, 3), (-2, 1), (-2, 3), (0, 2), (1, 1), (1, 3),
        (-1, 1), (-1, 3), (2, 0), (-2, 0), (0, 1), (0, 3), (1, 0), (-1, 0),
    )
)


def silu_normed(hidden, gain):
    factor = lax.rsqrt(jnp.mean(hidden * hidden, axis=1, keepdims=True) + EPS)
    half = hidden * factor * (0.5 * gain)
    return (half + half * jnp.tanh(half)).astype(BF16)


def patches(lat_ref, pat_ref, s, t):
    late = 6 - 2 * t
    sub = lax.broadcasted_iota(jnp.int32, (8, 128), 0)
    lane = lax.broadcasted_iota(jnp.int32, (8, 128), 1)
    turned = []
    for q in range(5):
        row = jnp.clip(s - 2 + q, 0, SEQ - 1) - s + 2
        blocks = []
        for b in range(TM):
            x = lat_ref[row * TM + b].astype(F32)
            moved = pltpu.roll(x, late, 0)
            x = jnp.where(sub < late, jnp.broadcast_to(x[0:1], (8, 128)), moved)
            blocks.append([pltpu.roll(x, (128 - 16 * (m - 1)) % 128, 1) for m in range(8)])
        turned.append(blocks)

    def piece(q, c, up):
        b, m = c // 8, c % 8
        k = (m + 4) % 8 if up else m
        base = 64 if up else 0
        own = turned[q][b][k]
        if m == 0:
            other = turned[q][b - 1][k] if b else turned[q][0][(k + 1) % 8]
            own = jnp.where(lane < base + 16, other, own)
        if m == 7:
            other = turned[q][b + 1][k] if b < 3 else turned[q][3][(k + 7) % 8]
            own = jnp.where(lane >= base + 32, other, own)
        return own

    for q in range(5):
        for c in range(W):
            low = piece(q, c, False)
            if q < 4:
                high = jnp.where((lane >= 64) & (lane < 112), piece(q + 1, c, True), 0.0)
            else:
                high = jnp.zeros((8, 128), F32)
            pat_ref[q, pl.ds(c, 8, stride=W), :] = jnp.where(lane < 48, low, high)


def merged(taps):
    wide = {place: value.astype(F32) for place, value in taps.items()}
    total = [wide[j, 0] + wide[j, 1] + wide[j, 2] for j in range(3)]
    values = {
        (0, 0, 1): total[0],
        (0, 1, 0): wide[1, 0] + wide[2, 0],
        (0, 1, 1): total[1] + total[2],
        (0, 1, 2): wide[1, 2] + wide[2, 2],
        (1, 0, 0): wide[0, 0] + wide[1, 0],
        (1, 0, 1): total[0] + total[1],
        (1, 0, 2): wide[0, 2] + wide[1, 2],
        (1, 1, 1): total[2],
    }
    values.update({p: wide[tap] for p, tap in RAW.items()})
    return values


def add_timed_taps(raw, summed, rows, half):
    lanes = pl.ds(128 * half, 128)
    steps = [
        merged({(j, k): raw[i, j, k, rows, lanes] for j in range(3) for k in range(3)})
        for i in range(3)
    ]
    for p in PLACES:
        g0, g1, g2 = (step[p] for step in steps)
        outer = g0 + g2
        for n, value in enumerate((g0, outer + g1, outer - g1, g2)):
            if (n, p) in KEPT:
                summed[KEPT.index((n, p)), half, rows, :] = value.astype(BF16)


def timed_matrix(raw, summed, rp, b, n):
    parts = []
    for u in range(2):
        p = (rp, u, b)
        if (n, p) in KEPT:
            kept = KEPT.index((n, p))
            halves = [summed[kept, half] for half in range(summed.shape[1])]
            parts.append(jnp.concatenate(halves, axis=1))
        else:
            j, k = RAW[p]
            parts.append(raw[0 if n == 0 else 2, j, k])
    return jnp.concatenate(parts, axis=0)


def gather_kernel(
    x_hbm, w1_hbm, w2_hbm, w3_hbm,
    lat, w1, w2, w2s, w3, w3s,
    send_sem, recv_sem, own_sem, sem1, sem2, sem3,
):
    s, t = lax.axis_index("seq"), lax.axis_index("tm")

    def away(d, e):
        return (s + d, lax.rem(t + e, TM))

    def when_row(d):
        if d == 0:
            return lambda f: f()
        return pl.when(s + d >= 0 if d < 0 else s + d < SEQ)

    barrier = pltpu.get_barrier_semaphore()
    for d, e in PEERS:

        @when_row(d)
        def _():
            pl.semaphore_signal(barrier, inc=1, device_id=away(d, e), device_id_type=MESH)

    own = lat.at[2 * TM + t]
    own_copy = pltpu.make_async_copy(x_hbm, own, own_sem)
    own_copy.start()

    parts = [pl.ds(128 * i, 128) for i in range(C1 // 128)]
    copies2 = [
        pltpu.make_async_copy(
            w2_hbm.at[:, :, :, part, :], w2.at[:, :, :, part, :], sem2.at[i]
        )
        for i, part in enumerate(parts)
    ]
    copy1 = pltpu.make_async_copy(
        w1_hbm, w1.at[:, pl.ds(0, 3), pl.ds(0, 48), :], sem1
    )
    copy3 = pltpu.make_async_copy(w3_hbm, w3, sem3)
    for copy in copies2:
        copy.start(priority=1)
    for i in range(3):
        w1[i, 3] = jnp.zeros((64, C1), BF16)
        for j in range(3):
            w1[i, j, 48:64, :] = jnp.zeros((16, C1), BF16)
    copy1.start(priority=1)
    copy3.start(priority=1)

    rows = 1 + jnp.minimum(s, 2) + jnp.minimum(SEQ - 1 - s, 2)
    own_copy.wait()
    pl.semaphore_wait(barrier, TM * rows - 1)
    for d, e in PEERS:

        @when_row(d)
        def _():
            pltpu.make_async_remote_copy(
                src_ref=own,
                dst_ref=lat.at[(2 - d) * TM + t],
                send_sem=send_sem.at[2 + d],
                recv_sem=recv_sem.at[2 - d],
                device_id=away(d, e),
                device_id_type=MESH,
            ).start()

    def all_of(d):
        some = lat.at[pl.ds(0, TM if d else TM - 1)]
        return pltpu.make_async_remote_copy(
            src_ref=some,
            dst_ref=some,
            send_sem=send_sem.at[2 + d],
            recv_sem=recv_sem.at[2 + d],
            device_id=away(0, 1),
            device_id_type=MESH,
        )

    for i, copy in enumerate(copies2):
        copy.wait()

        @pl.loop(0, 128 // CHUNK)
        def _(n):
            rows = pl.ds(pl.multiple_of(128 * i + CHUNK * n, CHUNK), CHUNK)
            for half in range(2):
                add_timed_taps(w2, w2s, rows, half)

    copy3.wait()

    @pl.loop(0, C2 // CHUNK)
    def _(n):
        add_timed_taps(w3, w3s, pl.ds(pl.multiple_of(CHUNK * n, CHUNK), CHUNK), 0)

    copy1.wait()
    for d in (0, 1, -1, 2, -2):

        @when_row(d)
        def _():
            all_of(d).wait_send()

    for d in (0, 1, -1, 2, -2):

        @when_row(d)
        def _():
            all_of(d).wait_recv()


def timed_terms(d):
    half1, half2 = d[1] * 0.5, d[2] * 0.5
    return d[0] - d[2], half1 + half2, half2 - half1, d[1] - d[3]


def convolutions(
    s, t, lat, out_ref, pat, w1, w2, w2s, w3, w3s, b1_ref, g1_ref, b2_ref, g2_ref, b3_ref, x1, x2, o32, first
):
    patches(lat, pat, s, t)
    start = 4 if first else 0
    size = W * (6 - start)
    def first_hidden(r):
        cols = []
        for i in range(3):
            for two in (0, 2):
                at = W * (i + start)
                cols.append(pat[r + two, at : at + size, :].astype(BF16))
        lhs = jnp.concatenate(cols, axis=1)
        return jnp.dot(lhs, w1[...].reshape(768, C1), preferred_element_type=F32)

    kinds = (1, 3) if first else (0, 1, 2, 3)
    hidden = {r: first_hidden(r) for r in (1, 0, 2)}
    acts = {}
    for r in (1, 0, 2):
        act = silu_normed(hidden[r] + b1_ref[...], g1_ref[...])
        if r == 0:
            act = jnp.where(s == 0, acts[1], act)
        if r == 2:
            act = jnp.where(s == SEQ - 1, acts[1], act)
        acts[r] = act
        d = {k: act[W * (k - start) : W * (k - start) + W] for k in range(start, 6)}
        for k in range(first, start):
            d[k] = d[start]
        for f in range(first, 4, 2):
            terms = timed_terms([d[f + k] for k in range(4)])
            for n in kinds:
                x1[n, r, W // 2 * f : W // 2 * f + W, :] = terms[n]

    size = W * (4 - first) // 2
    lhs = {
        n: jnp.concatenate(
            [
                x1[n, u : u + 2, W // 2 * first : 2 * W, :].reshape(2 * size, C1)
                for u in range(2)
            ],
            axis=1,
        )
        for n in kinds
    }
    col = lax.broadcasted_iota(jnp.int32, (2 * size, 1), 0) % W

    def two_frames(rp, b):
        m = {
            n: jnp.dot(lhs[n], timed_matrix(w2, w2s, rp, b, n), preferred_element_type=F32)
            for n in kinds
        }
        if first:
            return m[1], m[1] - m[3]
        return m[0] + (m[1] + m[2]), (m[1] - m[2]) - m[3]

    acts = {}
    for rp in range(2):
        for later, (q0, qk, q2) in enumerate(zip(*[two_frames(rp, b) for b in range(3)])):
            qk = qk + b2_ref[...]
            even = qk + jnp.where(col == 0, 0.0, pltpu.roll(q0, 1, 0) - q0)
            odd = qk + jnp.where(col == W - 1, 0.0, pltpu.roll(q2, 2 * size - 1, 0) - q2)
            for p, value in enumerate((even, odd)):
                act = silu_normed(value, g2_ref[...])
                for row in range(2):
                    for f in range(first, 4, 2):
                        part = act[size * row + W // 2 * (f - first) :][:W]
                        acts[2 * row + 1 - rp, p, f + later] = part
        for slot, p in [(2 * row + 1 - rp, p) for row in range(2) for p in range(2)]:
            d = [acts[slot, p, f if f >= first else first] for f in range(4)]
            terms = timed_terms(d)
            for n in kinds:
                x2[n, slot, W * p : W * p + W, :] = terms[n]

    def row_terms(n, slot):
        value = x2[n, slot]
        if slot == 0:
            value = jnp.where(s == 0, x2[n, 1], value)
        if slot == 3:
            value = jnp.where(s == SEQ - 1, x2[n, 2], value)
        return value

    col = lax.broadcasted_iota(jnp.int32, (32, 1), 0)
    for rp in range(2):
        m = {}
        for n in kinds:
            lhs = jnp.concatenate(
                [
                    jnp.concatenate([row_terms(n, rp + u + row) for row in range(2)], axis=0)
                    for u in range(2)
                ],
                axis=1,
            )
            taps = jnp.concatenate([timed_matrix(w3, w3s, rp, b, n) for b in range(3)], axis=1)
            m[n] = jnp.dot(lhs, taps, preferred_element_type=F32)
        if first:
            frames = m[1], m[1] - m[3]
        else:
            frames = m[0] + (m[1] + m[2]), (m[1] - m[2]) - m[3]
        for f, res in enumerate(frames):
            for row in range(2):
                base = 64 * row
                (e0, ek, e2), (o0, ok, o2) = [
                    [
                        res[base + 32 * p : base + 32 * p + 32, C3 * b : C3 * b + C3]
                        for b in range(3)
                    ]
                    for p in range(2)
                ]
                ek = ek + b3_ref[...]
                ok = ok + b3_ref[...]
                values = (
                    ek + jnp.where(col == 0, 0.0, pltpu.roll(o0, 1, 0) - e0),
                    ek + (o2 - e2),
                    ok + (e0 - o0),
                    ok + jnp.where(col == W - 1, 0.0, pltpu.roll(e2, 31, 0) - o2),
                )
                for n, value in enumerate(values):
                    o32[f, 2 * row + rp, pl.ds(n, W, stride=4), :] = value
                out_ref[f, 2 * row + rp] = o32[f, 2 * row + rp].astype(BF16)

def decode_kernel(
    lat, w1, w2, w2s, w3, w3s, b1_ref, g1_ref, b2_ref, g2_ref, b3_ref,
    out_ref,
    pat, x1, x2, o32,
):
    s, t = lax.axis_index("seq"), lax.axis_index("tm")

    refs = (lat, out_ref, pat, w1, w2, w2s, w3, w3s, b1_ref, g1_ref, b2_ref, g2_ref, b3_ref, x1, x2, o32)

    @pl.when(t == 0)
    def _():
        convolutions(s, t, *refs, 2)

    @pl.when(t > 0)
    def _():
        convolutions(s, t, *refs, 0)


def per_device(latent, w1, b1, g1, w2, b2, g2, w3, b3):
    line = lambda v: v.reshape(1, -1)
    vmem = pl.BlockSpec(memory_space=pltpu.VMEM)
    hbm = pl.BlockSpec(memory_space=pltpu.HBM)
    in_hbm = lambda v: pltpu.with_memory_space_constraint(v, pltpu.HBM)
    kept = pl.pallas_call(
        gather_kernel,
        out_shape=[
            pltpu.VMEM((5 * TM, 8, 128), BF16),
            pltpu.VMEM((3, 4, 64, C1), BF16),
            pltpu.VMEM((3, 3, 3, C1, C2), BF16),
            pltpu.VMEM((len(KEPT), 2, C1, 128), BF16),
            pltpu.VMEM((3, 3, 3, C2, C3), BF16),
            pltpu.VMEM((len(KEPT), 1, C2, C3), BF16),
        ],
        in_specs=[hbm] * 4,
        out_specs=[vmem] * 6,
        scratch_shapes=[
            pltpu.SemaphoreType.DMA((5,)),
            pltpu.SemaphoreType.DMA((5,)),
            pltpu.SemaphoreType.DMA,
            pltpu.SemaphoreType.DMA,
            pltpu.SemaphoreType.DMA((C1 // 128,)),
            pltpu.SemaphoreType.DMA,
        ],
        compiler_params=pltpu.CompilerParams(
            collective_id=0, has_side_effects=True, vmem_limit_bytes=8 << 20
        ),
        name="gather",
    )(*map(in_hbm, (latent, w1.reshape(3, 3, 48, C1), w2, w3)))
    return pl.pallas_call(
        decode_kernel,
        out_shape=jax.ShapeDtypeStruct((2, 4, 128, C3), BF16),
        in_specs=[vmem] * 11,
        out_specs=vmem,
        scratch_shapes=[
            pltpu.VMEM((5, 8 * W, 128), F32),
            pltpu.VMEM((4, 3, 2 * W, C1), BF16),
            pltpu.VMEM((4, 4, 2 * W, C2), BF16),
            pltpu.VMEM((2, 4, 128, C3), F32),
        ],
        compiler_params=pltpu.CompilerParams(vmem_limit_bytes=24 << 20),
        name="decode",
    )(*kept, line(b1), line(g1), line(b2), line(g2), line(b3))


def solution(mesh):
    placed = (P(None, ("seq", "tm")), P(), P(), P(), P(), P(), P(), P(), P())
    return jax.shard_map(
        per_device,
        mesh=mesh,
        in_specs=placed,
        out_specs=P("tm", "seq", None, None),
        check_vma=False,
    )
```
